1024 devices in a mesh: ta: 4 (over x), gx: 32 (over z), gy: 8 (over y, core).
Axes of the slice: x: 4, y: 4, z: 32, core: 2. Of those that a mesh axis runs over, the one named last changes fastest.
Arguments:
- eigvecs: bfloat16 [4, 32, 16, 24, 3, 2, 128], P('ta', 'gx', 'gy'), may hold values from -6 to 6
- links: bfloat16 [4, 32, 16, 24, 3, 2, 3, 3], P('ta', 'gx', 'gy'), may hold values from -4 to 4
- op_dirs: int32 [8], replicated, may hold values from 0 to 6, as said below
- op_moms: int32 [8], replicated, may hold values from 0 to 2
- perams: bfloat16 [128, 2, 512, 512], P(('ta', 'gx')), may hold values from -0.25 to 0.25
- pair_times: int32 [128, 2], P(('ta', 'gx')), may hold values from 0 to 3
- slot_counts: int32 [128], P(('ta', 'gx')), may hold values from 1 to 1, as said below
Outputs:
- margins: float32 [4, 8, 2, 128, 128], P('ta', 'gy')
- correlators: float32 [128, 8, 2], P(('ta', 'gx'), 'gy')
The draws below stay inside these ranges and needn't reach their ends.
Inputs may be any that keep to these rules, and one draw needn't show every extreme that they name: Owner k holds slot k of the slot dimension; slot_counts[k] is 1 in every draw. `op_dirs`: codes 0, 1, 2 step forward along the first, second, third dimension, codes 3, 4, 5 step backward along them, code 6 is no displacement. Every code is used by some operator. `op_moms`: momentum in units of 2 pi / 24.
All inputs are finite; a program needn't handle non-finite values.
Results may differ from the reference program's by a relative error of at most 0.0061.
Values may be sent and summed in bfloat16 or wider, within the bound.
A program may use at most 32 MiB of HBM per device.

```python
import math
import jax
import jax.numpy as jnp
from jax import lax

NEV = 128
NOP = 8
LZ = 24
SLOTS = 1
NT = 4
LX = 32
LY = 16
OWNERS = 128
PERAMS = 128
DIM = 512


def draw_slot_counts(key, part):
    first_key, second_key, third_key = jax.random.split(jax.random.fold_in(key, 17), 3)
    first_draw = jax.random.randint(first_key, (OWNERS,), 0, SLOTS)
    second_draw = jax.random.randint(second_key, (OWNERS,), 0, SLOTS)
    slot_fill = 1 + jnp.minimum(first_draw, second_draw)
    busiest = jax.random.randint(third_key, (), 0, OWNERS)
    return jnp.where(jnp.arange(OWNERS) == busiest, SLOTS, slot_fill).astype(jnp.int32)


def draw_op_dirs(key, part):
    first_key, second_key, third_key = jax.random.split(jax.random.fold_in(key, 29), 3)
    every_code = jax.random.permutation(first_key, jnp.arange(7, dtype=jnp.int32))
    extra_codes = jax.random.randint(second_key, (NOP - 7,), 0, 7).astype(jnp.int32)
    listed = jnp.concatenate([every_code, extra_codes])
    order_keys = jax.random.permutation(third_key, jnp.arange(NOP, dtype=jnp.int32))
    return listed[order_keys].astype(jnp.int32)


def plant(values, own_key, smallest, top_value):
    index_at = [jax.random.randint(jax.random.fold_in(own_key, axis), (), 0, length) for axis, length in enumerate(values.shape)]
    longest = values.shape.index(max(values.shape))
    beside = index_at[:longest] + [(index_at[longest] + 1) % values.shape[longest]] + index_at[longest + 1:]
    return values.at[tuple(index_at)].set(smallest).at[tuple(beside)].set(top_value)


def shard_levels(rng, extent, shards, low, top_value):
    def one(axis_at, blocks):
        steps = jax.random.uniform(jax.random.fold_in(jax.random.fold_in(rng, 6), axis_at), (blocks,), jnp.float32, low / len(shards), top_value / len(shards))
        return jnp.repeat(jnp.exp(steps), extent[axis_at] // blocks).reshape((-1,) + (1,) * (len(extent) - axis_at - 1))

    factor_of = one(*shards[0])
    for cut in shards[1:]:
        factor_of = factor_of * one(*cut)
    return factor_of


def bell_draw(rng, extent, deviation, bound, shards=(), kind=jnp.bfloat16):
    result = deviation * jax.random.normal(rng, extent, jnp.float32)
    if shards:
        result = result * shard_levels(rng, extent, shards, -0.22, 0.18)
    return jnp.clip(result, -bound, bound).astype(kind)


def setup_inputs(seed: int = 0) -> dict:
    arg_keys = jax.random.split(jax.random.key(seed), 8)
    return {
        "eigvecs": bell_draw(arg_keys[0], (NT, LX, LY, LZ, 3, 2, NEV), 1.0, 6.0, ((0, 4), (1, 32), (2, 8))),
        "links": bell_draw(arg_keys[1], (NT, LX, LY, LZ, 3, 2, 3, 3), 0.41, 4.0, ((0, 4), (1, 32), (2, 8))),
        "op_dirs": draw_op_dirs(jax.random.fold_in(arg_keys[7], 71), 0),
        "op_moms": plant(jax.random.randint(arg_keys[3], (NOP,), 0, 3), jax.random.fold_in(arg_keys[3], 1), 0, 2).astype(jnp.int32),
        "perams": bell_draw(arg_keys[4], (PERAMS, 2, DIM, DIM), DIM ** -0.5, 0.25, ((0, 128),)),
        "pair_times": plant(jax.random.randint(arg_keys[5], (PERAMS, 2), 0, NT), jax.random.fold_in(arg_keys[5], 1), 0, NT - 1).astype(jnp.int32),
        "slot_counts": draw_slot_counts(jax.random.fold_in(arg_keys[7], 71), 0),
    }


def color_apply(link_dir, vec_field):
    link_real = link_dir[..., 0, :, :].astype(jnp.float32)
    link_imag = link_dir[..., 1, :, :].astype(jnp.float32)
    field_real = vec_field[..., :, 0, :].astype(jnp.float32)
    field_imag = vec_field[..., :, 1, :].astype(jnp.float32)
    real_part = jnp.einsum('...ab,...bn->...an', link_real, field_real) - jnp.einsum('...ab,...bn->...an', link_imag, field_imag)
    imag_part = jnp.einsum('...ab,...bn->...an', link_real, field_imag) + jnp.einsum('...ab,...bn->...an', link_imag, field_real)
    return jnp.stack([real_part, imag_part], axis=-2)

def color_adjoint(link_dir, vec_field):
    link_real = link_dir[..., 0, :, :].astype(jnp.float32)
    link_imag = link_dir[..., 1, :, :].astype(jnp.float32)
    field_real = vec_field[..., :, 0, :].astype(jnp.float32)
    field_imag = vec_field[..., :, 1, :].astype(jnp.float32)
    real_part = jnp.einsum('...ba,...bn->...an', link_real, field_real) + jnp.einsum('...ba,...bn->...an', link_imag, field_imag)
    imag_part = jnp.einsum('...ba,...bn->...an', link_real, field_imag) - jnp.einsum('...ba,...bn->...an', link_imag, field_real)
    return jnp.stack([real_part, imag_part], axis=-2)

def phase_turn(values, momentum, z_coord):
    angle = 2.0 * math.pi * momentum.astype(jnp.float32) * z_coord / z_coord.shape[0]
    cosine = jnp.cos(angle)[:, None, None]
    sine = jnp.sin(angle)[:, None, None]
    values_real = values[..., 0, :]
    values_imag = values[..., 1, :]
    return jnp.stack([cosine * values_real - sine * values_imag, sine * values_real + cosine * values_imag], axis=-2)

def margin_block(vec_field, displaced):
    vectors = vec_field.shape[-1]
    left_matrix = vec_field.reshape(-1, vectors)
    rotated = jnp.stack([displaced[..., 1, :], -displaced[..., 0, :]], axis=-2)
    right_matrix = jnp.concatenate([displaced.reshape(-1, vectors), rotated.reshape(-1, vectors)], axis=1)
    product = jnp.dot(left_matrix.T, right_matrix, preferred_element_type=jnp.float32)
    return product.reshape(vectors, 2, vectors).transpose(1, 0, 2)

def contract(tau_matrix, sink_margin, source_margin):
    order = tau_matrix.shape[-1]
    vectors = sink_margin.shape[-1]
    spins = order // vectors
    count_ops = sink_margin.shape[0]
    tau_real = tau_matrix[0].astype(jnp.float32)
    tau_imag = tau_matrix[1].astype(jnp.float32)
    sink_real = sink_margin[:, 0].astype(jnp.float32)
    sink_imag = sink_margin[:, 1].astype(jnp.float32)
    source_real = source_margin[:, 0].astype(jnp.float32)
    source_imag = source_margin[:, 1].astype(jnp.float32)
    rows_real = tau_real.reshape(spins, vectors, order)
    rows_imag = tau_imag.reshape(spins, vectors, order)
    left_real = jnp.einsum('oab,sbc->osac', sink_real, rows_real) - jnp.einsum('oab,sbc->osac', sink_imag, rows_imag)
    left_imag = jnp.einsum('oab,sbc->osac', sink_real, rows_imag) + jnp.einsum('oab,sbc->osac', sink_imag, rows_real)
    cols_real = tau_real.reshape(order, spins, vectors)
    cols_imag = tau_imag.reshape(order, spins, vectors)
    right_real = jnp.einsum('isd,ocd->oisc', cols_real, source_real) + jnp.einsum('isd,ocd->oisc', cols_imag, source_imag)
    right_imag = jnp.einsum('isd,ocd->oisc', cols_imag, source_real) - jnp.einsum('isd,ocd->oisc', cols_real, source_imag)
    left_real = left_real.reshape(count_ops, order, order)
    left_imag = left_imag.reshape(count_ops, order, order)
    right_real = right_real.reshape(count_ops, order, order)
    right_imag = right_imag.reshape(count_ops, order, order)
    trace_real = lax.optimization_barrier(jnp.sum(left_real * right_real + left_imag * right_imag, axis=(1, 2)))
    trace_imag = lax.optimization_barrier(jnp.sum(left_imag * right_real - left_real * right_imag, axis=(1, 2)))
    return jnp.stack([trace_real, trace_imag], axis=-1) / vectors

def make_branches():
    branches = []
    for d in range(3):
        branches.append(partial_forward(d))
    for d in range(3):
        branches.append(partial_backward(d))
    branches.append(lambda vec_field, link_time: vec_field.astype(jnp.float32))
    return branches

def partial_forward(d):

    def forward(vec_field, link_time):
        return color_apply(link_time[..., d, :, :, :], jnp.roll(vec_field, -1, axis=d))
    return forward

def partial_backward(d):

    def backward(vec_field, link_time):
        carried = color_adjoint(link_time[..., d, :, :, :], vec_field).astype(jnp.bfloat16)
        return jnp.roll(carried, 1, axis=d).astype(jnp.float32)
    return backward

def reference(eigvecs, links, op_dirs, op_moms, perams, pair_times, slot_counts):
    branches = make_branches()
    norm_factor = 1.0 / math.sqrt(3.0 * LX * LY * LZ)
    z_coord = jnp.arange(LZ, dtype=jnp.float32)

    def one_time(inputs):
        vec_field, link_time = inputs
        op_rows = []
        for o in range(NOP):
            moved = lax.switch(op_dirs[o], branches, vec_field, link_time)
            displaced = phase_turn(moved, op_moms[o], z_coord).astype(jnp.bfloat16)
            op_rows.append(margin_block(vec_field, displaced))
        return jnp.stack(op_rows) * norm_factor
    margins = lax.map(one_time, (eigvecs, links))
    margins_b = margins.astype(jnp.bfloat16)

    def one_slot(inputs):
        tau_matrix, pair_row, slot_index = inputs
        sink_margin = lax.dynamic_index_in_dim(margins_b, pair_row[0], 0, keepdims=False)
        source_margin = lax.dynamic_index_in_dim(margins_b, pair_row[1], 0, keepdims=False)
        slot_value = contract(tau_matrix, sink_margin, source_margin)
        is_live = slot_index % SLOTS < slot_counts[slot_index // SLOTS]
        return jnp.where(is_live, slot_value, jnp.zeros_like(slot_value))
    correlators = lax.map(one_slot, (perams, pair_times, jnp.arange(PERAMS, dtype=jnp.int32)))
    return (margins, correlators)
```

```python
import math

import jax
import jax.numpy as jnp
from jax import lax
from jax.experimental import pallas as pl
from jax.experimental.pallas import tpu as pltpu
from jax.sharding import PartitionSpec as P

MESH = pl.DeviceIdType.MESH
DELTAS = (-1, 0, 1, 2)
F32 = jnp.float32
BF16 = jnp.bfloat16


def iota(shape, dim):
    return lax.broadcasted_iota(jnp.int32, shape, dim)


def ones_where(cond):
    return jnp.where(cond, 1.0, 0.0).astype(F32)


def mm(a, b):
    return jnp.dot(a, b, preferred_element_type=F32)


def mm_nt(a, b):
    return lax.dot_general(a, b, (((1,), (1,)), ((), ())), preferred_element_type=F32)


def peers(sizes):
    n_ta, n_gx, n_gy = sizes
    wanted = [(0, -1, 0), (0, 0, -1)]
    wanted += [(0, delta, j) for j in range(n_gy) for delta in DELTAS]
    wanted += [(0, step, 0) for step in (2, -2)]
    if n_gx > 8:
        wanted += [(0, step, 0) for step in (4, -4)]
    wanted += [(jt, delta, 0) for jt in range(n_ta) for delta in DELTAS]
    seen = []
    for ta, gx, gy in wanted:
        at = (ta % n_ta, gx % n_gx, gy % n_gy)
        if at != (0, 0, 0) and at not in seen:
            seen.append(at)
    return seen


def kernel(
    sizes, cells_z, norm_factor,
    dirs_ref, moms_ref, pair_ref, v_ref, links_ref, perams_ref,
    margin_ref, corr_ref,
    tau_ref, halo_x, halo_y, field, turned, left, cos_ref, sin_ref, part, recv, total, relay_r, relay_l, every,
    tau_sem, halo_send, halo_recv, part_send, part_recv, relay_send, relay_recv, last_send, last_recv,
):
    n_ta, n_gx, n_gy = sizes
    ta, gx, gy = (lax.axis_index(axis) for axis in ("ta", "gx", "gy"))
    layer = cells_z * 6
    cells_y = v_ref.shape[0] // layer
    n_relay = n_gx // 8

    def device(dta, dgx, dgy):
        return {
            "ta": lax.rem(ta + dta % n_ta, n_ta),
            "gx": lax.rem(gx + dgx % n_gx, n_gx),
            "gy": lax.rem(gy + dgy % n_gy, n_gy),
        }

    def remote(src, dst, send_sem, recv_sem, *offset):
        return pltpu.make_async_remote_copy(
            src_ref=src, dst_ref=dst, send_sem=send_sem, recv_sem=recv_sem,
            device_id=device(*offset), device_id_type=MESH,
        )

    barrier = pltpu.get_barrier_semaphore()
    known = peers(sizes)
    for dta, dgx, dgy in known:
        pl.semaphore_signal(
            barrier, inc=1, device_id=device(-dta, -dgx, -dgy), device_id_type=MESH
        )
    tau_copy = pltpu.make_async_copy(perams_ref, tau_ref, tau_sem)
    tau_copy.start()

    pl.semaphore_wait(barrier, len(known))
    send_x = remote(v_ref, halo_x, halo_send.at[0], halo_recv.at[0], 0, -1, 0)
    send_y = remote(v_ref.at[pl.ds(0, layer)], halo_y, halo_send.at[1], halo_recv.at[1], 0, 0, -1)
    send_x.start()
    send_y.start()

    n_k = links_ref.shape[1]
    row = iota((layer, layer), 0)
    col = iota((layer, layer), 1)
    same_site = row // 6 == col // 6
    shift = ones_where(col == lax.rem(row + 6, layer)).astype(BF16)
    shift_back = ones_where(row == lax.rem(col + 6, layer)).astype(BF16)
    turn = (
        ones_where((row % 2 == 1) & (col == row - 1)) - ones_where((row % 2 == 0) & (col == row + 1))
    ).astype(BF16)
    pick = ones_where(iota((layer, cells_z), 0) // 6 == iota((layer, cells_z), 1))
    k_row = iota((layer, n_k), 0)
    k_col = iota((layer, n_k), 1)
    color_of_row = (k_row // 2) % 3
    keep_row = color_of_row == (k_col // 6) % 3
    keep_col = color_of_row == (k_col // 2) % 3
    k = iota((n_k, layer), 0)
    c = iota((n_k, layer), 1)
    even = row % 2 == 0

    z_coord = iota((cells_z, 128), 0).astype(F32)
    for mom in range(3):
        angle = (2.0 * math.pi * mom) * z_coord / cells_z
        cos_ref[mom] = jnp.dot(pick, jnp.cos(angle), precision=lax.Precision.HIGHEST, preferred_element_type=F32)
        sin_ref[mom] = jnp.dot(pick, jnp.sin(angle), precision=lax.Precision.HIGHEST, preferred_element_type=F32)

    def put(code, y, plain, rotated):
        field[code, pl.ds(y * layer, layer)] = plain
        turned[code, pl.ds(y * layer, layer)] = rotated

    pick_b = pick.astype(BF16)
    forward = []
    for y in range(cells_y):
        v_y = v_ref[pl.ds(y * layer, layer), :]
        v_turned = mm(turn, v_y)
        put(6, y, v_y.astype(F32), v_turned)
        entries = mm_nt(pick_b, links_ref[y])
        by_row = jnp.where(keep_row, entries, 0.0).astype(BF16)
        by_col = jnp.where(keep_col, entries, 0.0).astype(BF16)
        for d in range(3):
            in_d = k // 18 == d
            re_k, im_k = k % 2 == 0, k % 2 == 1
            re_c, im_c = c % 2 == 0, c % 2 == 1
            b_match = in_d & ((k // 2) % 3 == (c // 2) % 3)
            a_match = in_d & ((k // 6) % 3 == (c // 2) % 3)
            g_re = ones_where(b_match & re_c & re_k) - ones_where(b_match & im_c & im_k)
            g_im = ones_where(b_match & re_c & im_k) + ones_where(b_match & im_c & re_k)
            h_re = ones_where(a_match & re_c & re_k) + ones_where(a_match & im_c & im_k)
            h_im = ones_where(a_match & im_c & re_k) - ones_where(a_match & re_c & im_k)
            q_re = mm(by_row, g_re.astype(BF16))
            q_im = mm(by_row, g_im.astype(BF16))
            apply = jnp.where(same_site, jnp.where(even, q_re, q_im), 0.0).astype(BF16)
            apply_turned = jnp.where(same_site, jnp.where(even, -q_im, q_re), 0.0).astype(BF16)
            p_re = mm(by_col, h_re.astype(BF16))
            p_im = mm(by_col, h_im.astype(BF16))
            adjoint = jnp.where(same_site, jnp.where(even, p_re, p_im), 0.0).astype(BF16)
            carried = mm(adjoint, v_y).astype(BF16)
            if d == 2:
                carried = mm(shift_back, carried).astype(BF16)
                v_next = mm(shift, v_y).astype(BF16)
                put(2, y, mm(apply, v_next), mm(apply_turned, v_next))
            else:
                forward.append((d, y, apply, apply_turned))
            put(3 + d, y, carried.astype(F32), mm(turn, carried))

    vectors = v_ref.shape[1]
    unit = ones_where(iota((vectors, vectors), 0) == iota((vectors, vectors), 1)).astype(BF16)
    left[0] = mm_nt(unit, v_ref[...]).astype(BF16)

    send_y.wait_recv()
    send_x.wait_recv()
    v_y_next = [v_ref[pl.ds(y * layer, layer), :] for y in range(1, cells_y)] + [halo_y[...]]
    left[1] = mm_nt(unit, halo_x[...]).astype(BF16)
    left[2] = mm_nt(unit, jnp.concatenate(v_y_next, axis=0)).astype(BF16)
    for d, y, apply, apply_turned in forward:
        v_next = halo_x[pl.ds(y * layer, layer), :] if d == 0 else v_y_next[y]
        put(d, y, mm(apply, v_next), mm(apply_turned, v_next))

    chunk = vectors // 4
    sends = []
    for j in [i for i in (4, 5, 3, 2, 6, 1, 7, 0) if i < n_gy]:
        op = lax.rem(gy + j, n_gy)
        code = dirs_ref[op]
        mom = moms_ref[op]
        side = jnp.where(code == 3, 1, jnp.where(code == 4, 2, 0))
        cosine = jnp.concatenate([cos_ref[mom]] * cells_y, axis=0)
        sine = jnp.concatenate([sin_ref[mom]] * cells_y, axis=0)
        plain, rotated = field[code], turned[code]
        displaced = (cosine * plain + sine * rotated).astype(BF16)
        minus_turned = (sine * plain - cosine * rotated).astype(BF16)
        right = jnp.concatenate([displaced, minus_turned], axis=1)
        part[j] = mm(left[side], right).reshape(4, chunk, 2 * vectors)
        for i, delta in enumerate(DELTAS):
            if j == 0 and delta == 0:
                continue
            slot = j * 4 + i
            to_chunk = lax.rem(gx + delta % n_gx, 4)
            copy = remote(
                part.at[j, to_chunk], recv.at[slot], part_send.at[slot], part_recv.at[slot], 0, delta, j
            )
            copy.start()
            sends.append(copy)

    summed = part[0, lax.rem(gx, 4)]
    for copy, slot in zip(sends, [s for j in (4, 5, 3, 2, 6, 1, 7, 0) if j < n_gy for s in range(4 * j, 4 * j + 4) if s != 1]):
        copy.wait_recv()
        summed = summed + recv[slot]
    total[...] = summed

    relays = []
    for i in range(n_relay):
        step = 2 if i == 0 else 4
        for way, ring in ((1, relay_r), (-1, relay_l)):
            at = 2 * i + (way < 0)
            if i > 0:
                relays[2 * (i - 1) + (way < 0)].wait_recv()
            copy = remote(
                total if i == 0 else ring.at[i - 1], ring.at[i], relay_send.at[at], relay_recv.at[at], 0, way * step, 0
            )
            copy.start()
            relays.append(copy)
    relays[-2].wait_recv()
    relays[-1].wait_recv()
    final = relay_r[0] + relay_l[0]
    for i in range(1, n_relay):
        final = final + (relay_r[i] + relay_l[i])
    my_chunk = lax.rem(gx + 2, 4)
    every[ta, my_chunk] = (final * norm_factor).astype(BF16)

    lasts = []
    for jt in [i for i in (2, 1, 3, 0) if i < n_ta]:
        for i, delta in enumerate(DELTAS):
            if jt == 0 and delta == 0:
                continue
            slot = jt * 4 + i
            copy = remote(
                every.at[ta, my_chunk], every.at[ta, my_chunk], last_send.at[slot], last_recv.at[slot], jt, delta, 0
            )
            copy.start()
            lasts.append(copy)
    tau_copy.wait()
    for copy in lasts:
        copy.wait_recv()

    mine = every[ta].reshape(vectors, 2 * vectors).astype(F32)
    margin_ref[0] = mine[:, :vectors]
    margin_ref[1] = mine[:, vectors:]

    sink = every[pair_ref[0, 0]].reshape(vectors, 2 * vectors)
    source = every[pair_ref[0, 1]].reshape(vectors, 2 * vectors)
    sink_r, sink_i = sink[:, :vectors], sink[:, vectors:]
    source_r, source_i = source[:, :vectors], source[:, vectors:]
    phi = jnp.concatenate(
        [jnp.concatenate([sink_r, -sink_i], axis=1), jnp.concatenate([sink_i, sink_r], axis=1)], axis=0
    )
    psi = jnp.concatenate([source, jnp.concatenate([-source_i, source_r], axis=1)], axis=0)
    spins = tau_ref.shape[1] // vectors
    x_blocks = []
    for s in range(spins):
        rows = pl.ds(s * vectors, vectors)
        x_blocks.append(mm(phi, jnp.concatenate([tau_ref[0, rows, :], tau_ref[1, rows, :]], axis=0)))
    sum_re = jnp.zeros((vectors, vectors), F32)
    sum_im = jnp.zeros((vectors, vectors), F32)
    for t in range(spins):
        cols = pl.ds(t * vectors, vectors)
        y_block = mm_nt(jnp.concatenate([tau_ref[0, :, cols], tau_ref[1, :, cols]], axis=1), psi)
        for s in range(spins):
            x_re = x_blocks[s][:vectors, t * vectors : (t + 1) * vectors]
            x_im = x_blocks[s][vectors:, t * vectors : (t + 1) * vectors]
            y_re = y_block[s * vectors : (s + 1) * vectors, :vectors]
            y_im = y_block[s * vectors : (s + 1) * vectors, vectors:]
            sum_re = sum_re + (x_re * y_re + x_im * y_im)
            sum_im = sum_im + (x_im * y_re - x_re * y_im)
    corr_ref[0, 0] = jnp.sum(sum_re) / vectors
    corr_ref[0, 1] = jnp.sum(sum_im) / vectors

    for copy in [send_x, send_y] + sends + relays + lasts:
        copy.wait_send()


def solution(mesh):
    sizes = tuple(mesh.shape[axis] for axis in ("ta", "gx", "gy"))

    def per_device(eigvecs, links, op_dirs, op_moms, perams, pair_times, slot_counts):
        cells_x, cells_y, cells_z, colors, parts, vectors = eigvecs.shape[1:]
        rows = cells_x * cells_y * cells_z * colors * parts
        order = perams.shape[-1]
        n_k = 3 * 2 * 3 * 3
        field = eigvecs.reshape(rows, vectors)
        link_rows = links[0, 0].transpose(0, 2, 4, 5, 3, 1).reshape(cells_y, n_k, cells_z)
        norm_factor = 1.0 / math.sqrt(3.0 * cells_x * sizes[1] * cells_y * sizes[2] * cells_z)
        layer = rows // cells_y
        n_relay = sizes[1] // 8
        chunk = vectors // 4
        smem = pl.BlockSpec(memory_space=pltpu.SMEM)
        vmem = pl.BlockSpec(memory_space=pltpu.VMEM)
        dma = pltpu.SemaphoreType.DMA
        margins, corr = pl.pallas_call(
            lambda *refs: kernel(sizes, cells_z, norm_factor, *refs),
            name="meson_step",
            out_shape=(
                jax.ShapeDtypeStruct((2, vectors, vectors), F32),
                jax.ShapeDtypeStruct((1, 2), F32),
            ),
            in_specs=[smem, smem, smem, vmem, vmem, pl.BlockSpec(memory_space=pl.ANY)],
            out_specs=(vmem, smem),
            scratch_shapes=[
                pltpu.VMEM((2, order, order), BF16),
                pltpu.VMEM((rows, vectors), BF16),
                pltpu.VMEM((layer, vectors), BF16),
                pltpu.VMEM((7, rows, vectors), F32),
                pltpu.VMEM((7, rows, vectors), F32),
                pltpu.VMEM((3, vectors, rows), BF16),
                pltpu.VMEM((3, layer, vectors), F32),
                pltpu.VMEM((3, layer, vectors), F32),
                pltpu.VMEM((sizes[2], 4, chunk, 2 * vectors), F32),
                pltpu.VMEM((sizes[2] * 4, chunk, 2 * vectors), F32),
                pltpu.VMEM((chunk, 2 * vectors), F32),
                pltpu.VMEM((n_relay, chunk, 2 * vectors), F32),
                pltpu.VMEM((n_relay, chunk, 2 * vectors), F32),
                pltpu.VMEM((sizes[0], 4, chunk, 2 * vectors), BF16),
                dma,
                dma((2,)),
                dma((2,)),
                dma((sizes[2] * 4,)),
                dma((sizes[2] * 4,)),
                dma((2 * n_relay,)),
                dma((2 * n_relay,)),
                dma((sizes[0] * 4,)),
                dma((sizes[0] * 4,)),
            ],
            compiler_params=pltpu.CompilerParams(collective_id=0, has_side_effects=True),
        )(op_dirs, op_moms, pair_times, field, link_rows, perams[0])
        return margins[None, None], corr[None]

    placed = (
        P("ta", "gx", "gy", None, None, None, None),
        P("ta", "gx", "gy", None, None, None, None, None),
        P(),
        P(),
        P(("ta", "gx"), None, None, None),
        P(("ta", "gx"), None),
        P(("ta", "gx")),
    )
    return jax.shard_map(
        per_device,
        mesh=mesh,
        in_specs=placed,
        out_specs=(P("ta", "gy", None, None, None), P(("ta", "gx"), "gy", None)),
        check_vma=False,
    )
```

```python
import math

import jax
import jax.numpy as jnp
from jax import lax
from jax.experimental import pallas as pl
from jax.experimental.pallas import tpu as pltpu
from jax.sharding import PartitionSpec as P

MESH = pl.DeviceIdType.MESH
DELTAS = (-1, 0, 1, 2)
WIDE = (-4, -3, -2, -1, 0, 1, 2, 3)
F32 = jnp.float32
BF16 = jnp.bfloat16


def iota(shape, dim):
    return lax.broadcasted_iota(jnp.int32, shape, dim)


def ones_where(cond):
    return jnp.where(cond, 1.0, 0.0).astype(F32)


def mm(a, b):
    return jnp.dot(a, b, preferred_element_type=F32)


def mm_nt(a, b):
    return lax.dot_general(a, b, (((1,), (1,)), ((), ())), preferred_element_type=F32)


def peers(sizes):
    n_ta, n_gx, n_gy = sizes
    wanted = [(0, -1, 0), (0, 0, -1)]
    wanted += [(0, 0, step) for step in (2, -2)]
    wanted += [(0, delta, step) for step in (0, 2, -2) for delta in DELTAS]
    wanted += [(0, step, 0) for step in (2, -2, 4, -4)]
    wanted += [(jt, delta, 0) for jt in range(n_ta) for delta in WIDE]
    seen = []
    for ta, gx, gy in wanted:
        at = (ta % n_ta, gx % n_gx, gy % n_gy)
        if at != (0, 0, 0) and at not in seen:
            seen.append(at)
    return seen


def kernel(
    sizes, cells_z, norm_factor,
    dirs_ref, moms_ref, pair_ref, v_hbm, links_hbm, perams_ref,
    margin_ref, corr_ref,
    tau_ref, v_ref, links_ref, entry_ref, halo_x, halo_y, field, turned, left, cos_ref, sin_ref,
    pair_out, pair_in, part, around_in, around, recv, total, half_in, window, far_in, every,
    local_sem, near_token, far_token, halo_send, halo_recv, pair_send, pair_recv, around_send, around_recv,
    part_send, part_recv, half_send, half_recv, far_send, far_recv, last_send, last_recv,
):
    n_ta, n_gx, n_gy = sizes
    ta, gx, gy = (lax.axis_index(axis) for axis in ("ta", "gx", "gy"))
    cells_y = links_ref.shape[0]
    layer = v_ref.shape[0] // cells_y
    core = lax.rem(gy, 2)
    flip = 1 - 2 * core
    far = n_gx >= 32

    def device(dta, dgx, dgy):
        return {
            "ta": lax.rem(ta + dta % n_ta, n_ta),
            "gx": lax.rem(gx + dgx % n_gx, n_gx),
            "gy": lax.rem(gy + dgy % n_gy, n_gy) if isinstance(dgy, int) else gy + dgy,
        }

    def remote(src, dst, send_sem, recv_sem, *offset):
        return pltpu.make_async_remote_copy(
            src_ref=src, dst_ref=dst, send_sem=send_sem, recv_sem=recv_sem,
            device_id=device(*offset), device_id_type=MESH,
        )

    barrier = pltpu.get_barrier_semaphore()
    known = peers(sizes)
    pl.semaphore_signal(barrier, inc=1, device_id=device(0, 0, flip), device_id_type=MESH)
    for dta, dgx, dgy in known:
        pl.semaphore_signal(
            barrier, inc=1, device_id=device(-dta, -dgx, -dgy), device_id_type=MESH
        )
    locals_ = [
        pltpu.make_async_copy(src, dst, local_sem.at[i])
        for i, (src, dst) in enumerate(
            ((links_hbm, links_ref), (v_hbm, v_ref), (perams_ref, tau_ref))
        )
    ]
    for copy in locals_:
        copy.start()
    locals_[0].wait()
    locals_[1].wait()

    pl.semaphore_wait(barrier, len(known) + 1)
    send_x = remote(v_ref, halo_x, halo_send.at[0], halo_recv.at[0], 0, -1, 0)
    send_y = remote(v_ref.at[pl.ds(0, layer)], halo_y, halo_send.at[1], halo_recv.at[1], 0, 0, -1)
    send_x.start()
    send_y.start()
    if far:
        for i, step in enumerate((4, -4)):
            pl.semaphore_signal(near_token.at[i], inc=1, device_id=device(0, step, 0), device_id_type=MESH)

    for y in range(cells_y):
        for k in range(links_ref.shape[1]):
            entry_ref[y, pl.ds(2 * k, 2), :] = links_ref[y, k].astype(F32)

    n_k = entry_ref.shape[1]
    row = iota((layer, layer), 0)
    col = iota((layer, layer), 1)
    same_site = row // 6 == col // 6
    shift = ones_where(col == lax.rem(row + 6, layer)).astype(BF16)
    shift_back = ones_where(row == lax.rem(col + 6, layer)).astype(BF16)
    turn = (
        ones_where((row % 2 == 1) & (col == row - 1)) - ones_where((row % 2 == 0) & (col == row + 1))
    ).astype(BF16)
    pick = ones_where(iota((layer, cells_z), 0) // 6 == iota((layer, cells_z), 1))
    k_row = iota((layer, n_k), 0)
    k_col = iota((layer, n_k), 1)
    color_of_row = (k_row // 2) % 3
    keep_row = color_of_row == (k_col // 6) % 3
    keep_col = color_of_row == (k_col // 2) % 3
    k = iota((n_k, layer), 0)
    c = iota((n_k, layer), 1)
    even = row % 2 == 0

    z_coord = iota((cells_z, 128), 0).astype(F32)
    for mom in range(3):
        angle = (2.0 * math.pi * mom) * z_coord / cells_z
        cos_ref[mom] = jnp.dot(pick, jnp.cos(angle), precision=lax.Precision.HIGHEST, preferred_element_type=F32)
        sin_ref[mom] = jnp.dot(pick, jnp.sin(angle), precision=lax.Precision.HIGHEST, preferred_element_type=F32)

    def put(code, y, plain, rotated):
        field[code, pl.ds(y * layer, layer)] = plain
        turned[code, pl.ds(y * layer, layer)] = rotated

    pick_b = pick.astype(BF16)
    forward = []
    for y in range(cells_y):
        v_y = v_ref[pl.ds(y * layer, layer), :]
        v_turned = mm(turn, v_y)
        put(6, y, v_y.astype(F32), v_turned)
        entries = mm_nt(pick_b, entry_ref[y].astype(BF16))
        by_row = jnp.where(keep_row, entries, 0.0).astype(BF16)
        by_col = jnp.where(keep_col, entries, 0.0).astype(BF16)
        for d in range(3):
            in_d = k // 18 == d
            re_k, im_k = k % 2 == 0, k % 2 == 1
            re_c, im_c = c % 2 == 0, c % 2 == 1
            b_match = in_d & ((k // 2) % 3 == (c // 2) % 3)
            a_match = in_d & ((k // 6) % 3 == (c // 2) % 3)
            g_re = ones_where(b_match & re_c & re_k) - ones_where(b_match & im_c & im_k)
            g_im = ones_where(b_match & re_c & im_k) + ones_where(b_match & im_c & re_k)
            h_re = ones_where(a_match & re_c & re_k) + ones_where(a_match & im_c & im_k)
            h_im = ones_where(a_match & im_c & re_k) - ones_where(a_match & re_c & im_k)
            q_re = mm(by_row, g_re.astype(BF16))
            q_im = mm(by_row, g_im.astype(BF16))
            apply = jnp.where(same_site, jnp.where(even, q_re, q_im), 0.0).astype(BF16)
            apply_turned = jnp.where(same_site, jnp.where(even, -q_im, q_re), 0.0).astype(BF16)
            p_re = mm(by_col, h_re.astype(BF16))
            p_im = mm(by_col, h_im.astype(BF16))
            adjoint = jnp.where(same_site, jnp.where(even, p_re, p_im), 0.0).astype(BF16)
            carried = mm(adjoint, v_y).astype(BF16)
            if d == 2:
                carried = mm(shift_back, carried).astype(BF16)
                v_next = mm(shift, v_y).astype(BF16)
                put(2, y, mm(apply, v_next), mm(apply_turned, v_next))
            else:
                forward.append((d, y, apply, apply_turned))
            put(3 + d, y, carried.astype(F32), mm(turn, carried))

    vectors = v_ref.shape[1]
    unit = ones_where(iota((vectors, vectors), 0) == iota((vectors, vectors), 1)).astype(BF16)
    left[0] = mm_nt(unit, v_ref[...]).astype(BF16)

    send_y.wait_recv()
    send_x.wait_recv()
    v_y_next = [v_ref[pl.ds(y * layer, layer), :] for y in range(1, cells_y)] + [halo_y[...]]
    left[1] = mm_nt(unit, halo_x[...]).astype(BF16)
    left[2] = mm_nt(unit, jnp.concatenate(v_y_next, axis=0)).astype(BF16)
    for d, y, apply, apply_turned in forward:
        v_next = halo_x[pl.ds(y * layer, layer), :] if d == 0 else v_y_next[y]
        put(d, y, mm(apply, v_next), mm(apply_turned, v_next))

    if far:
        for i, step in enumerate((4, -4)):
            pl.semaphore_wait(near_token.at[i], 1)
        for i, step in enumerate((8, -8)):
            pl.semaphore_signal(far_token.at[i], inc=1, device_id=device(0, step, 0), device_id_type=MESH)

    chunk = vectors // 4
    n_y = n_gy // 2
    row_y = gy // 2

    def margin(op):
        code = dirs_ref[op]
        mom = moms_ref[op]
        side = jnp.where(code == 3, 1, jnp.where(code == 4, 2, 0))
        cosine = jnp.concatenate([cos_ref[mom]] * cells_y, axis=0)
        sine = jnp.concatenate([sin_ref[mom]] * cells_y, axis=0)
        plain, rotated = field[code], turned[code]
        displaced = (cosine * plain + sine * rotated).astype(BF16)
        minus_turned = (sine * plain - cosine * rotated).astype(BF16)
        right = jnp.concatenate([displaced, minus_turned], axis=1)
        return mm(left[side], right).reshape(4, chunk, 2 * vectors)

    order = (2, 1, 3, 0)
    pairs = {}
    for k in order:
        pair_out[k] = margin(2 * lax.rem(row_y + k, n_y) + 1 - core)
        pairs[k] = remote(pair_out.at[k], pair_in.at[k], pair_send.at[k], pair_recv.at[k], 0, 0, flip)
        pairs[k].start()
    for k in order:
        part[k] = margin(2 * lax.rem(row_y + k, n_y) + core)

    def of(delta):
        return lax.rem(gx + delta % n_gx, 4)

    sends = {}

    def send_part(src, way, i):
        slot = way * 4 + i
        copy = remote(
            src, recv.at[slot], part_send.at[slot], part_recv.at[slot], 0, DELTAS[i], (0, 2, -2)[way]
        )
        copy.start()
        sends[slot] = copy

    arounds = []
    for k in order:
        pairs[k].wait_recv()
        part[k] = part[k] + pair_in[k]
        if k == 2:
            for i in range(4):
                copy = remote(
                    part.at[2, of(DELTAS[i])], around_in.at[i], around_send.at[i], around_recv.at[i], 0, 0, 2 if i < 2 else -2
                )
                copy.start()
                arounds.append(copy)
        elif k == 1:
            send_part(part.at[1, of(DELTAS[3])], 1, 3)
            send_part(part.at[1, of(DELTAS[2])], 1, 2)
        elif k == 3:
            send_part(part.at[3, of(DELTAS[0])], 2, 0)
            send_part(part.at[3, of(DELTAS[1])], 2, 1)
        else:
            for i in (3, 0, 2):
                send_part(part.at[0, of(DELTAS[i])], 0, i)
    for i in (0, 3, 1, 2):
        arounds[i].wait_recv()
        around[i] = part[1 if i < 2 else 3, of(DELTAS[i])] + around_in[i]
        send_part(around.at[i], 1 if i < 2 else 2, i)

    summed = part[0, of(0)]
    for slot in (3, 0, 2, 7, 6, 8, 9, 4, 11, 5, 10):
        sends[slot].wait_recv()
        summed = summed + recv[slot]
    total[...] = summed.reshape(2, chunk // 2, 2 * vectors)

    halves = []
    for i, step in enumerate((2, -2)):
        sub = lax.rem(lax.rem(gx + step % n_gx, n_gx) // 4, 2)
        copy = remote(total.at[sub], half_in.at[i], half_send.at[i], half_recv.at[i], 0, step, 0)
        copy.start()
        halves.append(copy)
    if far:
        for i in range(2):
            pl.semaphore_wait(far_token.at[i], 1)
    for copy in halves:
        copy.wait_recv()
    window[...] = half_in[0] + half_in[1]
    fars = []
    for i, step in enumerate((12, -12, 4, -4) if far else (4, -4)):
        copy = remote(window, far_in.at[i], far_send.at[i], far_recv.at[i], 0, step, 0)
        copy.start()
        fars.append(copy)
    for copy in fars[::-1]:
        copy.wait_recv()
    final = far_in[0] + far_in[1]
    for i in range(2, len(fars)):
        final = final + far_in[i]
    own = 2 * lax.rem(gx + 2, 4) + lax.rem(gx // 4 + 1, 2)
    every[ta, own] = (final * norm_factor).astype(BF16)

    lasts = []
    for jt in [i for i in (2, 1, 3, 0) if i < n_ta]:
        for i in (0, 1, 7, 2, 6, 3, 5, 4):
            if jt == 0 and WIDE[i] == 0:
                continue
            slot = jt * 8 + i
            copy = remote(
                every.at[ta, own], every.at[ta, own], last_send.at[slot], last_recv.at[slot], jt, WIDE[i], 0
            )
            copy.start()
            lasts.append(copy)
    locals_[2].wait()
    for copy in lasts:
        copy.wait_recv()

    mine = every[ta].reshape(vectors, 2 * vectors)
    margin_ref[0] = mine[:, :vectors]
    margin_ref[1] = mine[:, vectors:]

    sink = every[pair_ref[0, 0]].reshape(vectors, 2 * vectors)
    source = every[pair_ref[0, 1]].reshape(vectors, 2 * vectors)
    sink_r, sink_i = sink[:, :vectors], sink[:, vectors:]
    source_r, source_i = source[:, :vectors], source[:, vectors:]
    phi = jnp.concatenate(
        [jnp.concatenate([sink_r, -sink_i], axis=1), jnp.concatenate([sink_i, sink_r], axis=1)], axis=0
    )
    psi = jnp.concatenate([source, jnp.concatenate([-source_i, source_r], axis=1)], axis=0)
    spins = tau_ref.shape[1] // vectors
    x_blocks = []
    for s in range(spins):
        rows = pl.ds(s * vectors, vectors)
        x_blocks.append(mm(phi, jnp.concatenate([tau_ref[0, rows, :], tau_ref[1, rows, :]], axis=0)))
    sum_re = jnp.zeros((vectors, vectors), F32)
    sum_im = jnp.zeros((vectors, vectors), F32)
    for t in range(spins):
        cols = pl.ds(t * vectors, vectors)
        y_block = mm_nt(jnp.concatenate([tau_ref[0, :, cols], tau_ref[1, :, cols]], axis=1), psi)
        for s in range(spins):
            x_re = x_blocks[s][:vectors, t * vectors : (t + 1) * vectors]
            x_im = x_blocks[s][vectors:, t * vectors : (t + 1) * vectors]
            y_re = y_block[s * vectors : (s + 1) * vectors, :vectors]
            y_im = y_block[s * vectors : (s + 1) * vectors, vectors:]
            sum_re = sum_re + (x_re * y_re + x_im * y_im)
            sum_im = sum_im + (x_im * y_re - x_re * y_im)
    corr_ref[0, 0] = jnp.sum(sum_re) / vectors
    corr_ref[0, 1] = jnp.sum(sum_im) / vectors

    for copy in [send_x, send_y, *pairs.values(), *arounds, *sends.values(), *halves, *fars, *lasts]:
        copy.wait_send()


def solution(mesh):
    sizes = tuple(mesh.shape[axis] for axis in ("ta", "gx", "gy"))

    def per_device(eigvecs, links, op_dirs, op_moms, perams, pair_times, slot_counts):
        cells_x, cells_y, cells_z, colors, parts, vectors = eigvecs.shape[1:]
        rows = cells_x * cells_y * cells_z * colors * parts
        order = perams.shape[-1]
        n_k = 3 * 2 * 3 * 3
        field = eigvecs.reshape(rows, vectors)
        link_rows = links[0, 0].transpose(0, 2, 4, 5, 3, 1).reshape(cells_y, n_k // 2, 2, cells_z)
        norm_factor = 1.0 / math.sqrt(3.0 * cells_x * sizes[1] * cells_y * sizes[2] * cells_z)
        layer = rows // cells_y
        n_far = 4 if sizes[1] >= 32 else 2
        chunk = vectors // 4
        piece = (chunk, 2 * vectors)
        half = (chunk // 2, 2 * vectors)
        smem = pl.BlockSpec(memory_space=pltpu.SMEM)
        vmem = pl.BlockSpec(memory_space=pltpu.VMEM)
        hbm = pl.BlockSpec(memory_space=pl.ANY)
        dma = pltpu.SemaphoreType.DMA
        margins, corr = pl.pallas_call(
            lambda *refs: kernel(sizes, cells_z, norm_factor, *refs),
            name="meson_step",
            out_shape=(
                jax.ShapeDtypeStruct((2, vectors, vectors), BF16),
                jax.ShapeDtypeStruct((1, 2), F32),
            ),
            in_specs=[smem, smem, smem, hbm, hbm, hbm],
            out_specs=(vmem, smem),
            scratch_shapes=[
                pltpu.VMEM((2, order, order), BF16),
                pltpu.VMEM((rows, vectors), BF16),
                pltpu.VMEM((cells_y, n_k // 2, 2, cells_z), BF16),
                pltpu.VMEM((cells_y, n_k, cells_z), F32),
                pltpu.VMEM((rows, vectors), BF16),
                pltpu.VMEM((layer, vectors), BF16),
                pltpu.VMEM((7, rows, vectors), F32),
                pltpu.VMEM((7, rows, vectors), F32),
                pltpu.VMEM((3, vectors, rows), BF16),
                pltpu.VMEM((3, layer, vectors), F32),
                pltpu.VMEM((3, layer, vectors), F32),
                pltpu.VMEM((4, 4, *piece), F32),
                pltpu.VMEM((4, 4, *piece), F32),
                pltpu.VMEM((4, 4, *piece), F32),
                pltpu.VMEM((4, *piece), F32),
                pltpu.VMEM((4, *piece), F32),
                pltpu.VMEM((12, *piece), F32),
                pltpu.VMEM((2, *half), F32),
                pltpu.VMEM((2, *half), F32),
                pltpu.VMEM(half, F32),
                pltpu.VMEM((n_far, *half), F32),
                pltpu.VMEM((sizes[0], 8, *half), BF16),
                dma((3,)),
                pltpu.SemaphoreType.REGULAR((2,)),
                pltpu.SemaphoreType.REGULAR((2,)),
                dma((2,)),
                dma((2,)),
                dma((4,)),
                dma((4,)),
                dma((4,)),
                dma((4,)),
                dma((12,)),
                dma((12,)),
                dma((2,)),
                dma((2,)),
                dma((n_far,)),
                dma((n_far,)),
                dma((sizes[0] * 8,)),
                dma((sizes[0] * 8,)),
            ],
            compiler_params=pltpu.CompilerParams(collective_id=0, has_side_effects=True),
        )(op_dirs, op_moms, pair_times, field, link_rows, perams[0])
        return margins.astype(F32)[None, None], corr[None]

    placed = (
        P("ta", "gx", "gy", None, None, None, None),
        P("ta", "gx", "gy", None, None, None, None, None),
        P(),
        P(),
        P(("ta", "gx"), None, None, None),
        P(("ta", "gx"), None),
        P(("ta", "gx")),
    )
    return jax.shard_map(
        per_device,
        mesh=mesh,
        in_specs=placed,
        out_specs=(P("ta", "gy", None, None, None), P(("ta", "gx"), "gy", None)),
        check_vma=False,
    )
```

```python
import math

import jax
import jax.numpy as jnp
from jax import lax
from jax.experimental import pallas as pl
from jax.experimental.pallas import tpu as pltpu
from jax.sharding import PartitionSpec as P

MESH = pl.DeviceIdType.MESH
DELTAS = (-1, 0, 1, 2)
WIDE = (-4, -3, -2, -1, 0, 1, 2, 3)
F32 = jnp.float32
BF16 = jnp.bfloat16


def iota(shape, dim):
    return lax.broadcasted_iota(jnp.int32, shape, dim)


def ones_where(cond):
    return jnp.where(cond, 1.0, 0.0).astype(F32)


def mm(a, b):
    return jnp.dot(a, b, preferred_element_type=F32)


def mm_nt(a, b):
    return lax.dot_general(a, b, (((1,), (1,)), ((), ())), preferred_element_type=F32)


def peers(sizes):
    n_ta, n_gx, n_gy = sizes
    wanted = [(0, -1, 0), (0, 1, 0), (0, 0, -1), (0, 0, 2), (0, 0, -2), (1, 0, 0), (-1, 0, 0)]
    seen = []
    for ta, gx, gy in wanted:
        at = (ta % n_ta, gx % n_gx, gy % n_gy)
        if at != (0, 0, 0) and at not in seen:
            seen.append(at)
    return seen


def kernel(
    sizes, cells_z, norm_factor,
    dirs_ref, moms_ref, pair_ref, v_hbm, links_hbm, perams_ref,
    margin_ref, corr_ref,
    tau_ref, v_ref, links_ref, entry_ref, halo_x, field, turned, left, cos_ref, sin_ref,
    part, around_in, around, recv, total, half_in, window, far_in, every,
    local_sem, token, halo_send, halo_recv, around_send, around_recv,
    part_send, part_recv, half_send, half_recv, far_send, far_recv, last_send, last_recv,
):
    n_ta, n_gx, n_gy = sizes
    ta, gx, gy = (lax.axis_index(axis) for axis in ("ta", "gx", "gy"))
    cells_y = links_ref.shape[1]
    rows = v_hbm.shape[0]
    layer = rows // cells_y
    core = lax.rem(gy, 2)
    flip = 1 - 2 * core
    far = n_gx >= 32
    mine_at = pl.ds(pl.multiple_of(core * rows, rows), rows)

    def device(dta, dgx, dgy):
        return {
            "ta": lax.rem(ta + dta % n_ta, n_ta),
            "gx": lax.rem(gx + dgx % n_gx, n_gx),
            "gy": lax.rem(gy + dgy % n_gy, n_gy) if isinstance(dgy, int) else gy + dgy,
        }

    def remote(src, dst, send_sem, recv_sem, *offset):
        return pltpu.make_async_remote_copy(
            src_ref=src, dst_ref=dst, send_sem=send_sem, recv_sem=recv_sem,
            device_id=device(*offset), device_id_type=MESH,
        )

    barrier = pltpu.get_barrier_semaphore()
    known = peers(sizes)
    for dgx in (0, 1):
        pl.semaphore_signal(barrier, inc=1, device_id=device(0, dgx, flip), device_id_type=MESH)
    for dta, dgx, dgy in known:
        pl.semaphore_signal(
            barrier, inc=1, device_id=device(-dta, -dgx, -dgy), device_id_type=MESH
        )
    locals_ = [
        pltpu.make_async_copy(src, dst, local_sem.at[i])
        for i, (src, dst) in enumerate(
            ((links_hbm, links_ref.at[core]), (v_hbm, v_ref.at[mine_at]), (perams_ref, tau_ref))
        )
    ]
    for copy in locals_:
        copy.start()
    n_k = entry_ref.shape[0]
    row = iota((layer, layer), 0)
    col = iota((layer, layer), 1)
    same_site = row // 6 == col // 6
    shift = ones_where(col == lax.rem(row + 6, layer)).astype(BF16)
    shift_back = ones_where(row == lax.rem(col + 6, layer)).astype(BF16)
    turn = (
        ones_where((row % 2 == 1) & (col == row - 1)) - ones_where((row % 2 == 0) & (col == row + 1))
    ).astype(BF16)
    pick = ones_where(iota((layer, cells_z), 0) // 6 == iota((layer, cells_z), 1))
    k_row = iota((layer, n_k), 0)
    k_col = iota((layer, n_k), 1)
    color_of_row = (k_row // 2) % 3
    keep_row = color_of_row == (k_col // 6) % 3
    keep_col = color_of_row == (k_col // 2) % 3
    k = iota((n_k, layer), 0)
    c = iota((n_k, layer), 1)
    even = row % 2 == 0

    z_coord = iota((cells_z, 128), 0).astype(F32)
    for mom in range(3):
        angle = (2.0 * math.pi * mom) * z_coord / cells_z
        cos_ref[mom] = jnp.dot(pick, jnp.cos(angle), precision=lax.Precision.HIGHEST, preferred_element_type=F32)
        sin_ref[mom] = jnp.dot(pick, jnp.sin(angle), precision=lax.Precision.HIGHEST, preferred_element_type=F32)

    def put(code, at, plain, rotated):
        field[code, at] = plain
        turned[code, at] = rotated

    maps = []
    for d in range(3):
        in_d = k // 18 == d
        re_k, im_k = k % 2 == 0, k % 2 == 1
        re_c, im_c = c % 2 == 0, c % 2 == 1
        b_match = in_d & ((k // 2) % 3 == (c // 2) % 3)
        a_match = in_d & ((k // 6) % 3 == (c // 2) % 3)
        g_re = ones_where(b_match & re_c & re_k) - ones_where(b_match & im_c & im_k)
        g_im = ones_where(b_match & re_c & im_k) + ones_where(b_match & im_c & re_k)
        h_re = ones_where(a_match & re_c & re_k) + ones_where(a_match & im_c & im_k)
        h_im = ones_where(a_match & im_c & re_k) - ones_where(a_match & re_c & im_k)
        maps.append([m.astype(BF16) for m in (g_re, g_im, h_re, h_im)])

    pl.semaphore_wait(barrier, len(known) + 2)
    halos = [
        remote(v_hbm, halo_x.at[mine_at], halo_send.at[0], halo_recv.at[0], 0, -1, 0),
        remote(v_hbm, v_ref.at[mine_at], halo_send.at[1], halo_recv.at[1], 0, 0, flip),
        remote(links_hbm, links_ref.at[core], halo_send.at[2], halo_recv.at[2], 0, 0, flip),
        remote(v_hbm, halo_x.at[mine_at], halo_send.at[3], halo_recv.at[3], 0, -1, flip),
    ]
    edge = v_hbm.at[pl.ds(0, layer)]
    edge_to = v_ref.at[pl.ds(2 * rows, layer)]
    edges = [
        remote(edge, edge_to, halo_send.at[4 + i], halo_recv.at[4], 0, 0, step)
        for i, step in enumerate((-1, -2))
    ]
    for copy in halos:
        copy.start()

    @pl.when(core == 0)
    def _():
        for copy in edges:
            copy.start()

    ring = {"a": (0, 1), "b": (2, 2)}
    if far:
        ring |= {"c": (4, 4), "d": (6, 8)}
    side_ways = {"e": 8, "f": 10} if n_ta > 1 else {}

    def tell(name):
        if name in ring:
            at, step = ring[name]
            to = [(at, (0, step, 0)), (at + 1, (0, -step, 0))]
        else:
            to = [(side_ways[name] + i, (way, 0, 0)) for i, way in enumerate((1, -1))] if side_ways else []
        for at, offset in to:
            pl.semaphore_signal(token.at[at], inc=1, device_id=device(*offset), device_id_type=MESH)

    def heard(name):
        if name in ring or side_ways:
            at = ring[name][0] if name in ring else side_ways[name]
            pl.semaphore_wait(token.at[at], 1)
            pl.semaphore_wait(token.at[at + 1], 1)

    tell("a")

    pick_b = pick.astype(BF16)
    forward = []
    for own in (True, False):
        if own:
            locals_[0].wait()
            locals_[1].wait()
        else:
            heard("a")
            tell("b")
            halos[1].wait_recv()
            halos[2].wait_recv()
        whose = core if own else 1 - core
        for y in range(cells_y):
            at = pl.ds(pl.multiple_of(whose * rows + y * layer, layer), layer)
            after = pl.ds(pl.multiple_of(whose * rows + (y + 1) * layer, layer), layer)
            for kk in range(links_ref.shape[2]):
                entry_ref[pl.ds(2 * kk, 2), :] = links_ref[whose, y, kk].astype(F32)
            v_y = v_ref[at, :]
            put(6, at, v_y.astype(F32), mm(turn, v_y))
            entries = mm_nt(pick_b, entry_ref[...].astype(BF16))
            by_row = jnp.where(keep_row, entries, 0.0).astype(BF16)
            by_col = jnp.where(keep_col, entries, 0.0).astype(BF16)
            for d in range(3):
                g_re, g_im, h_re, h_im = maps[d]
                q_re = mm(by_row, g_re)
                q_im = mm(by_row, g_im)
                apply = jnp.where(same_site, jnp.where(even, q_re, q_im), 0.0).astype(BF16)
                apply_turned = jnp.where(same_site, jnp.where(even, -q_im, q_re), 0.0).astype(BF16)
                p_re = mm(by_col, h_re)
                p_im = mm(by_col, h_im)
                adjoint = jnp.where(same_site, jnp.where(even, p_re, p_im), 0.0).astype(BF16)
                carried = mm(adjoint, v_y).astype(BF16)
                if d == 2:
                    carried = mm(shift_back, carried).astype(BF16)
                    v_next = mm(shift, v_y).astype(BF16)
                    put(2, at, mm(apply, v_next), mm(apply_turned, v_next))
                else:
                    forward.append((d, at, after, apply, apply_turned))
                put(3 + d, at, carried.astype(F32), mm(turn, carried))

    vectors = v_ref.shape[1]
    unit = ones_where(iota((vectors, vectors), 0) == iota((vectors, vectors), 1)).astype(BF16)
    left[0] = mm_nt(unit, v_ref[pl.ds(0, 2 * rows), :]).astype(BF16)

    edges[0].wait_recv()
    left[2] = mm_nt(unit, v_ref[pl.ds(layer, 2 * rows), :]).astype(BF16)
    for d, at, after, apply, apply_turned in forward:
        if d == 1:
            v_next = v_ref[after, :]
            put(1, at, mm(apply, v_next), mm(apply_turned, v_next))
    halos[0].wait_recv()
    halos[3].wait_recv()
    heard("b")
    if far:
        tell("c")
    tell("e")
    left[1] = mm_nt(unit, halo_x[...]).astype(BF16)
    for d, at, after, apply, apply_turned in forward:
        if d == 0:
            v_next = halo_x[at, :]
            put(0, at, mm(apply, v_next), mm(apply_turned, v_next))
    chunk = vectors // 4
    n_y = n_gy // 2
    row_y = gy // 2

    def margin(op):
        code = dirs_ref[op]
        mom = moms_ref[op]
        side = jnp.where(code == 3, 1, jnp.where(code == 4, 2, 0))
        cosine = jnp.concatenate([cos_ref[mom]] * (2 * cells_y), axis=0)
        sine = jnp.concatenate([sin_ref[mom]] * (2 * cells_y), axis=0)
        plain, rotated = field[code], turned[code]
        displaced = (cosine * plain + sine * rotated).astype(BF16)
        minus_turned = (sine * plain - cosine * rotated).astype(BF16)
        right = jnp.concatenate([displaced, minus_turned], axis=1)
        return mm(left[side], right).reshape(4, chunk, 2 * vectors)

    order = (2, 1, 3, 0)

    def of(delta):
        return lax.rem(gx + delta % n_gx, 4)

    sends = {}

    def send_part(src, way, i):
        slot = way * 4 + i
        copy = remote(
            src, recv.at[slot], part_send.at[slot], part_recv.at[slot], 0, DELTAS[i], (0, 2, -2)[way]
        )
        copy.start()
        sends[slot] = copy

    arounds = []
    for k in order:
        part[k] = margin(2 * lax.rem(row_y + k, n_y) + core)
        if k == 2:
            for i in range(4):
                copy = remote(
                    part.at[2, of(DELTAS[i])], around_in.at[i], around_send.at[i], around_recv.at[i], 0, 0, 2 if i < 2 else -2
                )
                copy.start()
                arounds.append(copy)
        elif k == 1:
            send_part(part.at[1, of(DELTAS[3])], 1, 3)
            send_part(part.at[1, of(DELTAS[2])], 1, 2)
        elif k == 3:
            send_part(part.at[3, of(DELTAS[0])], 2, 0)
            send_part(part.at[3, of(DELTAS[1])], 2, 1)
        else:
            for i in (3, 0, 2):
                send_part(part.at[0, of(DELTAS[i])], 0, i)
    if far:
        heard("c")
        tell("d")
    heard("e")
    tell("f")
    for i in (0, 3, 1, 2):
        arounds[i].wait_recv()
        around[i] = part[1 if i < 2 else 3, of(DELTAS[i])] + around_in[i]
        send_part(around.at[i], 1 if i < 2 else 2, i)

    summed = part[0, of(0)]
    for slot in (3, 0, 2, 7, 6, 8, 9, 4, 11, 5, 10):
        sends[slot].wait_recv()
        summed = summed + recv[slot]
    total[...] = summed.reshape(2, chunk // 2, 2 * vectors)

    halves = []
    for i, step in enumerate((2, -2)):
        sub = lax.rem(lax.rem(gx + step % n_gx, n_gx) // 4, 2)
        copy = remote(total.at[sub], half_in.at[i], half_send.at[i], half_recv.at[i], 0, step, 0)
        copy.start()
        halves.append(copy)
    if far:
        heard("d")
    for copy in halves:
        copy.wait_recv()
    window[...] = half_in[0] + half_in[1]
    fars = []
    for i, step in enumerate((12, -12, 4, -4) if far else (4, -4)):
        copy = remote(window, far_in.at[i], far_send.at[i], far_recv.at[i], 0, step, 0)
        copy.start()
        fars.append(copy)
    for copy in fars[::-1]:
        copy.wait_recv()
    final = far_in[0] + far_in[1]
    for i in range(2, len(fars)):
        final = final + far_in[i]
    own = 2 * lax.rem(gx + 2, 4) + lax.rem(gx // 4 + 1, 2)
    every[ta, own] = (final * norm_factor).astype(BF16)

    heard("f")
    lasts = []
    for jt in [i for i in (2, 1, 3, 0) if i < n_ta]:
        for i in (0, 1, 7, 2, 6, 3, 5, 4):
            if jt == 0 and WIDE[i] == 0:
                continue
            slot = jt * 8 + i
            copy = remote(
                every.at[ta, own], every.at[ta, own], last_send.at[slot], last_recv.at[slot], jt, WIDE[i], 0
            )
            copy.start()
            lasts.append(copy)
    locals_[2].wait()
    for copy in lasts:
        copy.wait_recv()

    mine = every[ta].reshape(vectors, 2 * vectors)
    margin_ref[0] = mine[:, :vectors]
    margin_ref[1] = mine[:, vectors:]

    sink = every[pair_ref[0, 0]].reshape(vectors, 2 * vectors)
    source = every[pair_ref[0, 1]].reshape(vectors, 2 * vectors)
    sink_r, sink_i = sink[:, :vectors], sink[:, vectors:]
    source_r, source_i = source[:, :vectors], source[:, vectors:]
    phi = jnp.concatenate(
        [jnp.concatenate([sink_r, -sink_i], axis=1), jnp.concatenate([sink_i, sink_r], axis=1)], axis=0
    )
    psi = jnp.concatenate([source, jnp.concatenate([-source_i, source_r], axis=1)], axis=0)
    spins = tau_ref.shape[1] // vectors
    x_blocks = []
    for s in range(spins):
        rows = pl.ds(s * vectors, vectors)
        x_blocks.append(mm(phi, jnp.concatenate([tau_ref[0, rows, :], tau_ref[1, rows, :]], axis=0)))
    sum_re = jnp.zeros((vectors, vectors), F32)
    sum_im = jnp.zeros((vectors, vectors), F32)
    for t in range(spins):
        cols = pl.ds(t * vectors, vectors)
        y_block = mm_nt(jnp.concatenate([tau_ref[0, :, cols], tau_ref[1, :, cols]], axis=1), psi)
        for s in range(spins):
            x_re = x_blocks[s][:vectors, t * vectors : (t + 1) * vectors]
            x_im = x_blocks[s][vectors:, t * vectors : (t + 1) * vectors]
            y_re = y_block[s * vectors : (s + 1) * vectors, :vectors]
            y_im = y_block[s * vectors : (s + 1) * vectors, vectors:]
            sum_re = sum_re + (x_re * y_re + x_im * y_im)
            sum_im = sum_im + (x_im * y_re - x_re * y_im)
    corr_ref[0, 0] = jnp.sum(sum_re) / vectors
    corr_ref[0, 1] = jnp.sum(sum_im) / vectors

    for copy in [*halos, *arounds, *sends.values(), *halves, *fars, *lasts]:
        copy.wait_send()

    @pl.when(core == 0)
    def _():
        for copy in edges:
            copy.wait_send()


def solution(mesh):
    sizes = tuple(mesh.shape[axis] for axis in ("ta", "gx", "gy"))

    def per_device(eigvecs, links, op_dirs, op_moms, perams, pair_times, slot_counts):
        cells_x, cells_y, cells_z, colors, parts, vectors = eigvecs.shape[1:]
        rows = cells_x * cells_y * cells_z * colors * parts
        order = perams.shape[-1]
        n_k = 3 * 2 * 3 * 3
        field = eigvecs.reshape(rows, vectors)
        link_rows = links[0, 0].transpose(0, 2, 4, 5, 3, 1).reshape(cells_y, n_k // 2, 2, cells_z)
        norm_factor = 1.0 / math.sqrt(3.0 * cells_x * sizes[1] * cells_y * sizes[2] * cells_z)
        layer = rows // cells_y
        n_far = 4 if sizes[1] >= 32 else 2
        chunk = vectors // 4
        piece = (chunk, 2 * vectors)
        half = (chunk // 2, 2 * vectors)
        smem = pl.BlockSpec(memory_space=pltpu.SMEM)
        vmem = pl.BlockSpec(memory_space=pltpu.VMEM)
        hbm = pl.BlockSpec(memory_space=pltpu.HBM)
        dma = pltpu.SemaphoreType.DMA
        margins, corr = pl.pallas_call(
            lambda *refs: kernel(sizes, cells_z, norm_factor, *refs),
            name="meson_step",
            out_shape=(
                pltpu.VMEM((2, vectors, vectors), BF16),
                jax.ShapeDtypeStruct((1, 2), F32),
            ),
            in_specs=[smem, smem, smem, hbm, hbm, hbm],
            out_specs=(vmem, smem),
            scratch_shapes=[
                pltpu.VMEM((2, order, order), BF16),
                pltpu.VMEM((2 * rows + layer, vectors), BF16),
                pltpu.VMEM((2, cells_y, n_k // 2, 2, cells_z), BF16),
                pltpu.VMEM((n_k, cells_z), F32),
                pltpu.VMEM((2 * rows, vectors), BF16),
                pltpu.VMEM((7, 2 * rows, vectors), F32),
                pltpu.VMEM((7, 2 * rows, vectors), F32),
                pltpu.VMEM((3, vectors, 2 * rows), BF16),
                pltpu.VMEM((3, layer, vectors), F32),
                pltpu.VMEM((3, layer, vectors), F32),
                pltpu.VMEM((4, 4, *piece), F32),
                pltpu.VMEM((4, *piece), F32),
                pltpu.VMEM((4, *piece), F32),
                pltpu.VMEM((12, *piece), F32),
                pltpu.VMEM((2, *half), F32),
                pltpu.VMEM((2, *half), F32),
                pltpu.VMEM(half, F32),
                pltpu.VMEM((n_far, *half), F32),
                pltpu.VMEM((sizes[0], 8, *half), BF16),
                dma((3,)),
                pltpu.SemaphoreType.REGULAR((12,)),
                dma((6,)),
                dma((5,)),
                dma((4,)),
                dma((4,)),
                dma((12,)),
                dma((12,)),
                dma((2,)),
                dma((2,)),
                dma((n_far,)),
                dma((n_far,)),
                dma((sizes[0] * 8,)),
                dma((sizes[0] * 8,)),
            ],
            compiler_params=pltpu.CompilerParams(collective_id=0, has_side_effects=True, vmem_limit_bytes=56000 * 1024),
        )(op_dirs, op_moms, pair_times, field, link_rows, perams[0])
        return margins.astype(F32)[None, None], corr[None]

    placed = (
        P("ta", "gx", "gy", None, None, None, None),
        P("ta", "gx", "gy", None, None, None, None, None),
        P(),
        P(),
        P(("ta", "gx"), None, None, None),
        P(("ta", "gx"), None),
        P(("ta", "gx")),
    )
    return jax.shard_map(
        per_device,
        mesh=mesh,
        in_specs=placed,
        out_specs=(P("ta", "gy", None, None, None), P(("ta", "gx"), "gy", None)),
        check_vma=False,
    )
```

```python
import math

import jax
import jax.numpy as jnp
import numpy as np
from jax import lax
from jax.experimental import pallas as pl
from jax.experimental.pallas import tpu as pltpu
from jax.sharding import PartitionSpec as P

MESH = pl.DeviceIdType.MESH
DELTAS = (-1, 0, 1, 2)
WIDE = (-4, -3, -2, -1, 0, 1, 2, 3)
F32 = jnp.float32
BF16 = jnp.bfloat16


def mm(a, b):
    return jnp.dot(a, b, preferred_element_type=F32)


def mm_nt(a, b):
    return lax.dot_general(a, b, (((1,), (1,)), ((), ())), preferred_element_type=F32)


def phases(cells_z, vectors):
    angle = 2.0 * math.pi * np.arange(3)[:, None] * np.repeat(np.arange(cells_z), 6)[None] / cells_z
    return [np.repeat(f(angle)[..., None], vectors, axis=2) for f in (np.cos, np.sin)]


def selections(cells_z, vectors):
    layer, block, n_k = cells_z * 6, 48, 54
    at = np.arange(layer)
    shift = at[None] == (at[:, None] + 6) % layer
    r = np.arange(block)
    turn = ((r[:, None] % 2 == 1) & (r[None] == r[:, None] - 1)) * 1.0
    turn = turn - ((r[:, None] % 2 == 0) & (r[None] == r[:, None] + 1))
    same_site = (at[:, None] % block) // 6 == r[None] // 6
    pick = at[:, None] // 6 == np.arange(cells_z)[None]
    k = np.arange(2 * n_k) % n_k
    first = (np.arange(2 * n_k) < n_k)[None]
    even = (at % 2 == 0)[:, None]
    color = (at // 2 % 3)[:, None]
    keep_row, keep_col = color == (k // 6 % 3)[None], color == (k // 2 % 3)[None]
    row_plain = keep_row & (even == first)
    row_turned = (keep_row & first & ~even) * 1.0 - (keep_row & ~first & even)
    col_plain = keep_col & (even == first)
    maps = []
    k, first, c = k[:, None], first.T, r[None]
    re_k, im_k, re_c, im_c = k % 2 == 0, k % 2 == 1, c % 2 == 0, c % 2 == 1
    for d in range(3):
        b_match = (k // 18 == d) & (k // 2 % 3 == c // 2 % 3)
        a_match = (k // 18 == d) & (k // 6 % 3 == c // 2 % 3)
        g_re = (b_match & re_c & re_k) * 1.0 - (b_match & im_c & im_k)
        g_im = (b_match & re_c & im_k) * 1.0 + (b_match & im_c & re_k)
        h_re = (a_match & re_c & re_k) * 1.0 + (a_match & im_c & im_k)
        h_im = (a_match & im_c & re_k) * 1.0 - (a_match & re_c & im_k)
        maps += [np.where(first, g_re, g_im), np.where(first, h_re, h_im)]
    tables = [turn, shift, shift.T, same_site, pick, row_plain, row_turned, col_plain, np.eye(vectors), *maps]
    return [np.asarray(t, np.float32) for t in tables]


def peers(sizes):
    n_ta, n_gx, n_gy = sizes
    wanted = [(0, -1, 0), (0, 1, 0), (0, 0, -1), (0, 0, 2), (0, 0, -2), (1, 0, 0), (-1, 0, 0)]
    seen = []
    for ta, gx, gy in wanted:
        at = (ta % n_ta, gx % n_gx, gy % n_gy)
        if at != (0, 0, 0) and at not in seen:
            seen.append(at)
    return seen


def kernel(
    sizes, n_tables, norm_factor,
    dirs_hbm, moms_hbm, pair_hbm, v_hbm, links_hbm, perams_ref, *rest,
):
    sources, (margin_ref, corr_ref) = rest[:n_tables], rest[n_tables : n_tables + 2]
    tables, rest = rest[n_tables + 2 : 2 * n_tables + 2], rest[2 * n_tables + 2 :]
    (
        tau_ref, v_ref, links_ref, entry_ref, halo_x, field, turned, left, part, around_in, around, recv, total, half_in, window, far_in, every, local_sem, token, halo_send, halo_recv, around_send, around_recv, part_send, part_recv, half_send, half_recv, far_send, far_recv, last_send, last_recv,
        table_sem, dirs_ref, moms_ref, pair_ref, small_sem,
    ) = rest
    n_ta, n_gx, n_gy = sizes
    ta, gx, gy = (lax.axis_index(axis) for axis in ("ta", "gx", "gy"))
    cells_y = links_ref.shape[1]
    rows = v_hbm.shape[0]
    layer = rows // cells_y
    core = lax.rem(gy, 2)
    flip = 1 - 2 * core
    far = n_gx >= 32
    mine_at = pl.ds(pl.multiple_of(core * rows, rows), rows)

    def device(dta, dgx, dgy):
        return {
            "ta": lax.rem(ta + dta % n_ta, n_ta),
            "gx": lax.rem(gx + dgx % n_gx, n_gx),
            "gy": lax.rem(gy + dgy % n_gy, n_gy) if isinstance(dgy, int) else gy + dgy,
        }

    def remote(src, dst, send_sem, recv_sem, *offset):
        return pltpu.make_async_remote_copy(
            src_ref=src, dst_ref=dst, send_sem=send_sem, recv_sem=recv_sem,
            device_id=device(*offset), device_id_type=MESH,
        )

    barrier = pltpu.get_barrier_semaphore()
    known = peers(sizes)
    for dgx in (0, 1):
        pl.semaphore_signal(barrier, inc=1, device_id=device(0, dgx, flip), device_id_type=MESH)
    for dta, dgx, dgy in known:
        pl.semaphore_signal(
            barrier, inc=1, device_id=device(-dta, -dgx, -dgy), device_id_type=MESH
        )
    locals_ = [
        pltpu.make_async_copy(src, dst, local_sem.at[i])
        for i, (src, dst) in enumerate(
            ((links_hbm, links_ref.at[core]), (v_hbm, v_ref.at[mine_at]), (perams_ref, tau_ref))
        )
    ]
    table_copies = [
        pltpu.make_async_copy(src, dst, table_sem.at[i])
        for i, (src, dst) in enumerate(zip(sources, tables))
    ]
    smalls = [
        pltpu.make_async_copy(src, dst, small_sem.at[i])
        for i, (src, dst) in enumerate(
            ((dirs_hbm, dirs_ref), (moms_hbm, moms_ref), (pair_hbm, pair_ref))
        )
    ]
    for copy in locals_[:2] + table_copies + smalls + locals_[2:]:
        copy.start()
    turn, shift, shift_back, same_site, pick_b, row_plain, row_turned, col_plain, unit, *maps = (
        ref for ref in tables[: len(tables) - 2]
    )
    cos_ref, sin_ref = tables[-2:]
    n_k = maps[0].shape[0] // 2
    block = turn.shape[0]

    def put(code, at, plain, rotated):
        field[code, pl.ds(*at)] = plain
        turned[code, pl.ds(*at)] = rotated

    def part_of(x, i):
        return x[i * block : (i + 1) * block]

    pl.semaphore_wait(barrier, len(known) + 2)
    halos = [
        remote(v_hbm, halo_x.at[mine_at], halo_send.at[0], halo_recv.at[0], 0, -1, 0),
        remote(v_hbm, v_ref.at[mine_at], halo_send.at[1], halo_recv.at[1], 0, 0, flip),
        remote(links_hbm, links_ref.at[core], halo_send.at[2], halo_recv.at[2], 0, 0, flip),
        remote(v_hbm, halo_x.at[mine_at], halo_send.at[3], halo_recv.at[3], 0, -1, flip),
    ]
    edge = v_hbm.at[pl.ds(0, layer)]
    edge_to = v_ref.at[pl.ds(2 * rows, layer)]
    edges = [
        remote(edge, edge_to, halo_send.at[4 + i], halo_recv.at[4], 0, 0, step)
        for i, step in enumerate((-1, -2))
    ]
    for copy in halos:
        copy.start()

    @pl.when(core == 0)
    def _():
        for copy in edges:
            copy.start()

    ring = {"a": (0, 1), "b": (2, 2)}
    if far:
        ring |= {"c": (4, 4), "d": (6, 8)}
    side_ways = {"e": 8, "f": 10} if n_ta > 1 else {}

    def tell(name):
        if name in ring:
            at, step = ring[name]
            to = [(at, (0, step, 0)), (at + 1, (0, -step, 0))]
        else:
            to = [(side_ways[name] + i, (way, 0, 0)) for i, way in enumerate((1, -1))] if side_ways else []
        for at, offset in to:
            pl.semaphore_signal(token.at[at], inc=1, device_id=device(*offset), device_id_type=MESH)

    def heard(name):
        if name in ring or side_ways:
            at = ring[name][0] if name in ring else side_ways[name]
            pl.semaphore_wait(token.at[at], 1)
            pl.semaphore_wait(token.at[at + 1], 1)

    tell("a")

    forward = []
    for own in (True, False):
        if own:
            for copy in locals_[:2] + table_copies + smalls:
                copy.wait()
        else:
            heard("a")
            tell("b")
            halos[1].wait_recv()
            halos[2].wait_recv()
        whose = core if own else 1 - core
        base = pl.multiple_of(whose * rows, rows)
        spots = [(pl.multiple_of(base + i * block, block), block) for i in range(rows // block)]
        after = [(pl.multiple_of(base + layer + i * block, block), block) for i in range(rows // block)]
        lists = []
        for y in range(cells_y):
            for kk in range(links_ref.shape[2]):
                entry = links_ref[whose, y, kk].astype(F32)
                entry_ref[2 * own + y, pl.ds(2 * kk, 2), :] = entry
                entry_ref[2 * own + y, pl.ds(n_k + 2 * kk, 2), :] = entry
            lists.append(mm_nt(pick_b[...], entry_ref[2 * own + y].astype(BF16)).astype(BF16))
        by_row = jnp.concatenate([x * row_plain[...] for x in lists], axis=0)
        by_row_turned = jnp.concatenate([x * row_turned[...] for x in lists], axis=0)
        by_col = jnp.concatenate([x * col_plain[...] for x in lists], axis=0)
        site = jnp.concatenate([same_site[...]] * cells_y, axis=0)
        apply, apply_turned, adjoint = [], [], []
        for d in range(3):
            apply.append(mm(by_row, maps[2 * d][...]).astype(BF16) * site)
            apply_turned.append(mm(by_row_turned, maps[2 * d][...]).astype(BF16) * site)
            adjoint.append(mm(by_col, maps[2 * d + 1][...]).astype(BF16) * site)
        v_own = v_ref[pl.ds(base, rows), :]
        carried = [[], [], []]
        for i, spot in enumerate(spots):
            stack = jnp.concatenate([part_of(x, i) for x in adjoint] + [turn[...]], axis=0)
            product = mm(stack, part_of(v_own, i))
            put(6, spot, part_of(v_own, i).astype(F32), part_of(product, 3))
            for d in range(3):
                carried[d].append(part_of(product, d).astype(BF16))
        per = layer // block
        v_next, moved = [], []
        for y in range(cells_y):
            v_next.append(mm(shift[...], v_own[y * layer : (y + 1) * layer]).astype(BF16))
            moved.append(mm(shift_back[...], jnp.concatenate(carried[2][y * per : (y + 1) * per], axis=0)).astype(BF16))
        for i, spot in enumerate(spots):
            back = [carried[0][i], carried[1][i], part_of(moved[i // per], i % per)]
            back_turned = mm(turn[...], jnp.concatenate(back, axis=1))
            lanes = back[0].shape[1]
            for d in range(3):
                put(3 + d, spot, back[d].astype(F32), back_turned[:, d * lanes : (d + 1) * lanes])
                pair = jnp.concatenate([part_of(apply[d], i), part_of(apply_turned[d], i)], axis=0)
                if d == 2:
                    product = mm(pair, part_of(v_next[i // per], i % per))
                    put(2, spot, product[:block], product[block:])
                else:
                    forward.append((d, spot, after[i], pair))

    vectors = v_ref.shape[1]
    left[0] = mm_nt(unit[...], v_ref[pl.ds(0, 2 * rows), :]).astype(BF16)

    edges[0].wait_recv()
    left[2] = mm_nt(unit[...], v_ref[pl.ds(layer, 2 * rows), :]).astype(BF16)
    for d, at, after, pair in forward:
        if d == 1:
            product = mm(pair, v_ref[pl.ds(*after), :])
            put(1, at, product[:block], product[block:])
    halos[0].wait_recv()
    halos[3].wait_recv()
    heard("b")
    if far:
        tell("c")
    tell("e")
    left[1] = mm_nt(unit[...], halo_x[...]).astype(BF16)
    for d, at, after, pair in forward:
        if d == 0:
            product = mm(pair, halo_x[pl.ds(*at), :])
            put(0, at, product[:block], product[block:])
    chunk = vectors // 4
    n_y = n_gy // 2
    row_y = gy // 2

    def margin(op):
        code = dirs_ref[op]
        mom = moms_ref[op]
        side = jnp.where(code == 3, 1, jnp.where(code == 4, 2, 0))
        cosine = jnp.concatenate([cos_ref[mom]] * (2 * cells_y), axis=0)
        sine = jnp.concatenate([sin_ref[mom]] * (2 * cells_y), axis=0)
        plain, rotated = field[code], turned[code]
        displaced = (cosine * plain + sine * rotated).astype(BF16)
        minus_turned = (sine * plain - cosine * rotated).astype(BF16)
        right = jnp.concatenate([displaced, minus_turned], axis=1)
        return mm(left[side], right).reshape(4, chunk, 2 * vectors)

    order = (2, 1, 3, 0)

    def of(delta):
        return lax.rem(gx + delta % n_gx, 4)

    sends = {}

    def send_part(src, way, i):
        slot = way * 4 + i
        copy = remote(
            src, recv.at[slot], part_send.at[slot], part_recv.at[slot], 0, DELTAS[i], (0, 2, -2)[way]
        )
        copy.start()
        sends[slot] = copy

    arounds = []
    for k in order:
        part[k] = margin(2 * lax.rem(row_y + k, n_y) + core)
        if k == 2:
            for i in range(4):
                copy = remote(
                    part.at[2, of(DELTAS[i])], around_in.at[i], around_send.at[i], around_recv.at[i], 0, 0, 2 if i < 2 else -2
                )
                copy.start()
                arounds.append(copy)
        elif k == 1:
            send_part(part.at[1, of(DELTAS[3])], 1, 3)
            send_part(part.at[1, of(DELTAS[2])], 1, 2)
        elif k == 3:
            send_part(part.at[3, of(DELTAS[0])], 2, 0)
            send_part(part.at[3, of(DELTAS[1])], 2, 1)
        else:
            for i in (3, 0, 2):
                send_part(part.at[0, of(DELTAS[i])], 0, i)
    if far:
        heard("c")
        tell("d")
    heard("e")
    tell("f")
    for i in (0, 3, 1, 2):
        arounds[i].wait_recv()
        around[i] = part[1 if i < 2 else 3, of(DELTAS[i])] + around_in[i]
        send_part(around.at[i], 1 if i < 2 else 2, i)

    summed = part[0, of(0)]
    for slot in (3, 0, 2, 7, 6, 8, 9, 4, 11, 5, 10):
        sends[slot].wait_recv()
        summed = summed + recv[slot]
    total[...] = summed.reshape(2, chunk // 2, 2 * vectors)

    halves = []
    for i, step in enumerate((2, -2)):
        sub = lax.rem(lax.rem(gx + step % n_gx, n_gx) // 4, 2)
        copy = remote(total.at[sub], half_in.at[i], half_send.at[i], half_recv.at[i], 0, step, 0)
        copy.start()
        halves.append(copy)
    if far:
        heard("d")
    for copy in halves:
        copy.wait_recv()
    window[...] = half_in[0] + half_in[1]
    fars = []
    for i, step in enumerate((12, -12, 4, -4) if far else (4, -4)):
        copy = remote(window, far_in.at[i], far_send.at[i], far_recv.at[i], 0, step, 0)
        copy.start()
        fars.append(copy)
    for copy in fars[::-1]:
        copy.wait_recv()
    final = far_in[0] + far_in[1]
    for i in range(2, len(fars)):
        final = final + far_in[i]
    own = 2 * lax.rem(gx + 2, 4) + lax.rem(gx // 4 + 1, 2)
    every[ta, own] = (final * norm_factor).astype(BF16)

    heard("f")
    lasts = []
    for jt in [i for i in (2, 1, 3, 0) if i < n_ta]:
        for i in (0, 1, 7, 2, 6, 3, 5, 4):
            if jt == 0 and WIDE[i] == 0:
                continue
            slot = jt * 8 + i
            copy = remote(
                every.at[ta, own], every.at[ta, own], last_send.at[slot], last_recv.at[slot], jt, WIDE[i], 0
            )
            copy.start()
            lasts.append(copy)
    locals_[2].wait()
    for copy in lasts:
        copy.wait_recv()

    mine = every[ta].reshape(vectors, 2 * vectors)
    margin_ref[0] = mine[:, :vectors]
    margin_ref[1] = mine[:, vectors:]

    sink = every[pair_ref[0, 0]].reshape(vectors, 2 * vectors)
    source = every[pair_ref[0, 1]].reshape(vectors, 2 * vectors)
    sink_r, sink_i = sink[:, :vectors], sink[:, vectors:]
    source_r, source_i = source[:, :vectors], source[:, vectors:]
    phi = jnp.concatenate(
        [jnp.concatenate([sink_r, -sink_i], axis=1), jnp.concatenate([sink_i, sink_r], axis=1)], axis=0
    )
    psi = jnp.concatenate([source, jnp.concatenate([-source_i, source_r], axis=1)], axis=0)
    spins = tau_ref.shape[1] // vectors
    x_blocks = []
    for s in range(spins):
        rows = pl.ds(s * vectors, vectors)
        x_blocks.append(mm(phi, jnp.concatenate([tau_ref[0, rows, :], tau_ref[1, rows, :]], axis=0)))
    sum_re = jnp.zeros((vectors, vectors), F32)
    sum_im = jnp.zeros((vectors, vectors), F32)
    for t in range(spins):
        cols = pl.ds(t * vectors, vectors)
        y_block = mm_nt(jnp.concatenate([tau_ref[0, :, cols], tau_ref[1, :, cols]], axis=1), psi)
        for s in range(spins):
            x_re = x_blocks[s][:vectors, t * vectors : (t + 1) * vectors]
            x_im = x_blocks[s][vectors:, t * vectors : (t + 1) * vectors]
            y_re = y_block[s * vectors : (s + 1) * vectors, :vectors]
            y_im = y_block[s * vectors : (s + 1) * vectors, vectors:]
            sum_re = sum_re + (x_re * y_re + x_im * y_im)
            sum_im = sum_im + (x_im * y_re - x_re * y_im)
    traces = [jnp.sum(jnp.sum(x, axis=0, keepdims=True), axis=1, keepdims=True) for x in (sum_re, sum_im)]
    part_at = lax.broadcasted_iota(jnp.int32, (1, 2), 1)
    corr_ref[...] = jnp.where(part_at == 0, *traces) / vectors

    for copy in [*halos, *arounds, *sends.values(), *halves, *fars, *lasts]:
        copy.wait_send()

    @pl.when(core == 0)
    def _():
        for copy in edges:
            copy.wait_send()


def solution(mesh):
    sizes = tuple(mesh.shape[axis] for axis in ("ta", "gx", "gy"))

    def per_device(eigvecs, links, op_dirs, op_moms, perams, pair_times, slot_counts):
        cells_x, cells_y, cells_z, colors, parts, vectors = eigvecs.shape[1:]
        rows = cells_x * cells_y * cells_z * colors * parts
        order = perams.shape[-1]
        n_k = 3 * 2 * 3 * 3
        field = eigvecs.reshape(rows, vectors)
        link_rows = links[0, 0].transpose(0, 2, 4, 5, 3, 1).reshape(cells_y, n_k // 2, 2, cells_z)
        norm_factor = 1.0 / math.sqrt(3.0 * cells_x * sizes[1] * cells_y * sizes[2] * cells_z)
        layer = rows // cells_y
        n_far = 4 if sizes[1] >= 32 else 2
        chunk = vectors // 4
        piece = (chunk, 2 * vectors)
        half = (chunk // 2, 2 * vectors)
        tables = [jnp.asarray(t, BF16) for t in selections(cells_z, vectors)] + [jnp.asarray(t, F32) for t in phases(cells_z, vectors)]
        vmem = pl.BlockSpec(memory_space=pltpu.VMEM)
        hbm = pl.BlockSpec(memory_space=pltpu.HBM)
        dma = pltpu.SemaphoreType.DMA
        margins, corr = pl.pallas_call(
            lambda *refs: kernel(sizes, len(tables), norm_factor, *refs),
            name="meson_step",
            out_shape=(
                pltpu.VMEM((2, vectors, vectors), BF16),
                pltpu.VMEM((1, 2), F32),
            ),
            in_specs=[hbm] * (6 + len(tables)),
            out_specs=(vmem, vmem),
            scratch_shapes=[
                *(pltpu.VMEM(table.shape, table.dtype) for table in tables),
                pltpu.VMEM((2, order, order), BF16),
                pltpu.VMEM((2 * rows + layer, vectors), BF16),
                pltpu.VMEM((2, cells_y, n_k // 2, 2, cells_z), BF16),
                pltpu.VMEM((2 * cells_y, 2 * n_k, cells_z), F32),
                pltpu.VMEM((2 * rows, vectors), BF16),
                pltpu.VMEM((7, 2 * rows, vectors), F32),
                pltpu.VMEM((7, 2 * rows, vectors), F32),
                pltpu.VMEM((3, vectors, 2 * rows), BF16),
                pltpu.VMEM((4, 4, *piece), F32),
                pltpu.VMEM((4, *piece), F32),
                pltpu.VMEM((4, *piece), F32),
                pltpu.VMEM((12, *piece), F32),
                pltpu.VMEM((2, *half), F32),
                pltpu.VMEM((2, *half), F32),
                pltpu.VMEM(half, F32),
                pltpu.VMEM((n_far, *half), F32),
                pltpu.VMEM((sizes[0], 8, *half), BF16),
                dma((3,)),
                pltpu.SemaphoreType.REGULAR((12,)),
                dma((6,)),
                dma((5,)),
                dma((4,)),
                dma((4,)),
                dma((12,)),
                dma((12,)),
                dma((2,)),
                dma((2,)),
                dma((n_far,)),
                dma((n_far,)),
                dma((sizes[0] * 8,)),
                dma((sizes[0] * 8,)),
                dma((len(tables),)),
                pltpu.SMEM(op_dirs.shape, jnp.int32),
                pltpu.SMEM(op_moms.shape, jnp.int32),
                pltpu.SMEM(pair_times.shape, jnp.int32),
                dma((3,)),
            ],
            compiler_params=pltpu.CompilerParams(collective_id=0, has_side_effects=True, vmem_limit_bytes=56000 * 1024),
        )(op_dirs, op_moms, pair_times, field, link_rows, perams[0], *tables)
        return margins.astype(F32)[None, None], corr[None]

    placed = (
        P("ta", "gx", "gy", None, None, None, None),
        P("ta", "gx", "gy", None, None, None, None, None),
        P(),
        P(),
        P(("ta", "gx"), None, None, None),
        P(("ta", "gx"), None),
        P(("ta", "gx")),
    )
    return jax.shard_map(
        per_device,
        mesh=mesh,
        in_specs=placed,
        out_specs=(P("ta", "gy", None, None, None), P(("ta", "gx"), "gy", None)),
        check_vma=False,
    )
```

```python
import math

import jax
import jax.numpy as jnp
import numpy as np
from jax import lax
from jax.experimental import pallas as pl
from jax.experimental.pallas import tpu as pltpu
from jax.sharding import PartitionSpec as P

MESH = pl.DeviceIdType.MESH
DELTAS = (-1, 0, 1, 2)
WIDE = (-4, -3, -2, -1, 0, 1, 2, 3)
F32 = jnp.float32
BF16 = jnp.bfloat16


def mm(a, b):
    return jnp.dot(a, b, preferred_element_type=F32)


def mm_nt(a, b):
    return lax.dot_general(a, b, (((1,), (1,)), ((), ())), preferred_element_type=F32)


def phases(cells_z, vectors):
    angle = 2.0 * math.pi * np.arange(3)[:, None] * np.repeat(np.arange(cells_z), 6)[None] / cells_z
    return [np.repeat(f(angle)[..., None], vectors, axis=2) for f in (np.cos, np.sin)]


def selections(cells_z, vectors):
    layer, block, n_k = cells_z * 6, 48, 54
    at = np.arange(layer)
    shift = at[None] == (at[:, None] + 6) % layer
    r = np.arange(block)
    turn = ((r[:, None] % 2 == 1) & (r[None] == r[:, None] - 1)) * 1.0
    turn = turn - ((r[:, None] % 2 == 0) & (r[None] == r[:, None] + 1))
    same_site = (at[:, None] % block) // 6 == r[None] // 6
    pick = at[:, None] // 6 == np.arange(cells_z)[None]
    k = np.arange(2 * n_k) % n_k
    first = (np.arange(2 * n_k) < n_k)[None]
    even = (at % 2 == 0)[:, None]
    color = (at // 2 % 3)[:, None]
    keep_row, keep_col = color == (k // 6 % 3)[None], color == (k // 2 % 3)[None]
    row_plain = keep_row & (even == first)
    row_turned = (keep_row & first & ~even) * 1.0 - (keep_row & ~first & even)
    col_plain = keep_col & (even == first)
    maps = []
    k, first, c = k[:, None], first.T, r[None]
    re_k, im_k, re_c, im_c = k % 2 == 0, k % 2 == 1, c % 2 == 0, c % 2 == 1
    for d in range(3):
        b_match = (k // 18 == d) & (k // 2 % 3 == c // 2 % 3)
        a_match = (k // 18 == d) & (k // 6 % 3 == c // 2 % 3)
        g_re = (b_match & re_c & re_k) * 1.0 - (b_match & im_c & im_k)
        g_im = (b_match & re_c & im_k) * 1.0 + (b_match & im_c & re_k)
        h_re = (a_match & re_c & re_k) * 1.0 + (a_match & im_c & im_k)
        h_im = (a_match & im_c & re_k) * 1.0 - (a_match & re_c & im_k)
        maps += [np.where(first, g_re, g_im), np.where(first, h_re, h_im)]
    tables = [turn, shift, shift.T, same_site, pick, row_plain, row_turned, col_plain, np.eye(vectors), *maps]
    return [np.asarray(t, np.float32) for t in tables]


def peers(sizes):
    n_ta, n_gx, n_gy = sizes
    wanted = [(0, -1, 0), (0, 1, 0), (0, 0, -1), (0, 0, 2), (0, 0, -2), (1, 0, 0), (-1, 0, 0)]
    seen = []
    for ta, gx, gy in wanted:
        at = (ta % n_ta, gx % n_gx, gy % n_gy)
        if at != (0, 0, 0) and at not in seen:
            seen.append(at)
    return seen


def kernel(
    sizes, n_tables, norm_factor,
    dirs_hbm, moms_hbm, pair_hbm, v_hbm, links_hbm, perams_ref, *rest,
):
    sources, (margin_ref, corr_ref) = rest[:n_tables], rest[n_tables : n_tables + 2]
    tables, rest = rest[n_tables + 2 : 2 * n_tables + 2], rest[2 * n_tables + 2 :]
    (
        tau_ref, v_ref, links_ref, entry_ref, halo_x, field, turned, left, part, around_in, around, recv, total, half_in, window, far_in, every, local_sem, token, halo_send, halo_recv, around_send, around_recv, part_send, part_recv, half_send, half_recv, far_send, far_recv, last_send, last_recv,
        table_sem, dirs_ref, moms_ref, pair_ref, small_sem,
    ) = rest
    n_ta, n_gx, n_gy = sizes
    ta, gx, gy = (lax.axis_index(axis) for axis in ("ta", "gx", "gy"))
    cells_y = links_ref.shape[1]
    rows = v_hbm.shape[0]
    layer = rows // cells_y
    core = lax.rem(gy, 2)
    flip = 1 - 2 * core
    far = n_gx >= 32
    mine_at = pl.ds(pl.multiple_of(core * rows, rows), rows)

    def device(dta, dgx, dgy):
        return {
            "ta": lax.rem(ta + dta % n_ta, n_ta),
            "gx": lax.rem(gx + dgx % n_gx, n_gx),
            "gy": lax.rem(gy + dgy % n_gy, n_gy) if isinstance(dgy, int) else gy + dgy,
        }

    def remote(src, dst, send_sem, recv_sem, *offset):
        return pltpu.make_async_remote_copy(
            src_ref=src, dst_ref=dst, send_sem=send_sem, recv_sem=recv_sem,
            device_id=device(*offset), device_id_type=MESH,
        )

    barrier = pltpu.get_barrier_semaphore()
    known = peers(sizes)
    for dgx in (0, 1):
        pl.semaphore_signal(barrier, inc=1, device_id=device(0, dgx, flip), device_id_type=MESH)
    for dta, dgx, dgy in known:
        pl.semaphore_signal(
            barrier, inc=1, device_id=device(-dta, -dgx, -dgy), device_id_type=MESH
        )
    locals_ = [
        pltpu.make_async_copy(src, dst, local_sem.at[i])
        for i, (src, dst) in enumerate(
            ((links_hbm, links_ref.at[core]), (v_hbm, v_ref.at[mine_at]), (perams_ref, tau_ref))
        )
    ]
    table_copies = [
        pltpu.make_async_copy(src, dst, table_sem.at[i])
        for i, (src, dst) in enumerate(zip(sources, tables))
    ]
    smalls = [
        pltpu.make_async_copy(src, dst, small_sem.at[i])
        for i, (src, dst) in enumerate(
            ((dirs_hbm, dirs_ref), (moms_hbm, moms_ref), (pair_hbm, pair_ref))
        )
    ]
    for copy in locals_[:2] + table_copies + smalls + locals_[2:]:
        copy.start()
    turn, shift, shift_back, same_site, pick_b, row_plain, row_turned, col_plain, unit, *maps = (
        ref for ref in tables[: len(tables) - 2]
    )
    cos_ref, sin_ref = tables[-2:]
    n_k = maps[0].shape[0] // 2
    block = turn.shape[0]

    def put(code, at, plain, rotated):
        field[code, pl.ds(*at)] = plain
        turned[code, pl.ds(*at)] = rotated

    def part_of(x, i):
        return x[i * block : (i + 1) * block]

    pl.semaphore_wait(barrier, len(known) + 2)
    low = pl.ds(pl.multiple_of(core * rows, layer), layer)
    high = pl.ds(pl.multiple_of(core * rows + layer, layer), rows - layer)
    v_high = v_hbm.at[pl.ds(layer, rows - layer)]
    halos = [
        remote(v_hbm.at[pl.ds(0, layer)], halo_x.at[low], halo_send.at[0], halo_recv.at[0], 0, -1, 0),
        remote(v_hbm, v_ref.at[mine_at], halo_send.at[1], halo_recv.at[1], 0, 0, flip),
        remote(links_hbm, links_ref.at[core], halo_send.at[2], halo_recv.at[2], 0, 0, flip),
        remote(v_high, halo_x.at[high], halo_send.at[3], halo_recv.at[3], 0, -1, flip),
        remote(v_high, halo_x.at[high], halo_send.at[6], halo_recv.at[5], 0, -1, 0),
    ]
    passed = remote(halo_x.at[low], halo_x.at[low], halo_send.at[7], halo_recv.at[6], 0, 0, flip)
    edge = v_hbm.at[pl.ds(0, layer)]
    edge_to = v_ref.at[pl.ds(2 * rows, layer)]
    edges = [
        remote(edge, edge_to, halo_send.at[4 + i], halo_recv.at[4], 0, 0, step)
        for i, step in enumerate((-1, -2))
    ]
    for copy in halos:
        copy.start()

    @pl.when(core == 0)
    def _():
        for copy in edges:
            copy.start()

    ring = {"a": (0, 1), "b": (2, 2)}
    if far:
        ring |= {"c": (4, 4), "d": (6, 8)}
    side_ways = {"e": 8, "f": 10} if n_ta > 1 else {}

    def tell(name):
        if name in ring:
            at, step = ring[name]
            to = [(at, (0, step, 0)), (at + 1, (0, -step, 0))]
        else:
            to = [(side_ways[name] + i, (way, 0, 0)) for i, way in enumerate((1, -1))] if side_ways else []
        for at, offset in to:
            pl.semaphore_signal(token.at[at], inc=1, device_id=device(*offset), device_id_type=MESH)

    def heard(name):
        if name in ring or side_ways:
            at = ring[name][0] if name in ring else side_ways[name]
            pl.semaphore_wait(token.at[at], 1)
            pl.semaphore_wait(token.at[at + 1], 1)

    tell("a")

    forward = []
    for own in (True, False):
        if own:
            for copy in locals_[:2] + table_copies + smalls:
                copy.wait()
        else:
            heard("a")
            tell("b")
            halos[0].wait_recv()
            passed.start()
            halos[1].wait_recv()
            halos[2].wait_recv()
        whose = core if own else 1 - core
        base = pl.multiple_of(whose * rows, rows)
        spots = [(pl.multiple_of(base + i * block, block), block) for i in range(rows // block)]
        after = [(pl.multiple_of(base + layer + i * block, block), block) for i in range(rows // block)]
        lists = []
        for y in range(cells_y):
            for kk in range(links_ref.shape[2]):
                entry = links_ref[whose, y, kk].astype(F32)
                entry_ref[2 * own + y, pl.ds(2 * kk, 2), :] = entry
                entry_ref[2 * own + y, pl.ds(n_k + 2 * kk, 2), :] = entry
            lists.append(mm_nt(pick_b[...], entry_ref[2 * own + y].astype(BF16)).astype(BF16))
        by_row = jnp.concatenate([x * row_plain[...] for x in lists], axis=0)
        by_row_turned = jnp.concatenate([x * row_turned[...] for x in lists], axis=0)
        by_col = jnp.concatenate([x * col_plain[...] for x in lists], axis=0)
        site = jnp.concatenate([same_site[...]] * cells_y, axis=0)
        apply, apply_turned, adjoint = [], [], []
        for d in range(3):
            apply.append(mm(by_row, maps[2 * d][...]).astype(BF16) * site)
            apply_turned.append(mm(by_row_turned, maps[2 * d][...]).astype(BF16) * site)
            adjoint.append(mm(by_col, maps[2 * d + 1][...]).astype(BF16) * site)
        v_own = v_ref[pl.ds(base, rows), :]
        carried = [[], [], []]
        for i, spot in enumerate(spots):
            stack = jnp.concatenate([part_of(x, i) for x in adjoint] + [turn[...]], axis=0)
            product = mm(stack, part_of(v_own, i))
            put(6, spot, part_of(v_own, i).astype(F32), part_of(product, 3))
            for d in range(3):
                carried[d].append(part_of(product, d).astype(BF16))
        per = layer // block
        v_next, moved = [], []
        for y in range(cells_y):
            v_next.append(mm(shift[...], v_own[y * layer : (y + 1) * layer]).astype(BF16))
            moved.append(mm(shift_back[...], jnp.concatenate(carried[2][y * per : (y + 1) * per], axis=0)).astype(BF16))
        for i, spot in enumerate(spots):
            back = [carried[0][i], carried[1][i], part_of(moved[i // per], i % per)]
            back_turned = mm(turn[...], jnp.concatenate(back, axis=1))
            lanes = back[0].shape[1]
            for d in range(3):
                put(3 + d, spot, back[d].astype(F32), back_turned[:, d * lanes : (d + 1) * lanes])
                pair = jnp.concatenate([part_of(apply[d], i), part_of(apply_turned[d], i)], axis=0)
                if d == 2:
                    product = mm(pair, part_of(v_next[i // per], i % per))
                    put(2, spot, product[:block], product[block:])
                else:
                    forward.append((d, spot, after[i], pair))

    vectors = v_ref.shape[1]
    left[0] = mm_nt(unit[...], v_ref[pl.ds(0, 2 * rows), :]).astype(BF16)

    edges[0].wait_recv()
    left[2] = mm_nt(unit[...], v_ref[pl.ds(layer, 2 * rows), :]).astype(BF16)
    for d, at, after, pair in forward:
        if d == 1:
            product = mm(pair, v_ref[pl.ds(*after), :])
            put(1, at, product[:block], product[block:])
    for copy in (passed, *halos[3:]):
        copy.wait_recv()
    heard("b")
    if far:
        tell("c")
    tell("e")
    left[1] = mm_nt(unit[...], halo_x[...]).astype(BF16)
    for d, at, after, pair in forward:
        if d == 0:
            product = mm(pair, halo_x[pl.ds(*at), :])
            put(0, at, product[:block], product[block:])
    chunk = vectors // 4
    n_y = n_gy // 2
    row_y = gy // 2

    def margin(op):
        code = dirs_ref[op]
        mom = moms_ref[op]
        side = jnp.where(code == 3, 1, jnp.where(code == 4, 2, 0))
        cosine = jnp.concatenate([cos_ref[mom]] * (2 * cells_y), axis=0)
        sine = jnp.concatenate([sin_ref[mom]] * (2 * cells_y), axis=0)
        plain, rotated = field[code], turned[code]
        displaced = (cosine * plain + sine * rotated).astype(BF16)
        minus_turned = (sine * plain - cosine * rotated).astype(BF16)
        right = jnp.concatenate([displaced, minus_turned], axis=1)
        return mm(left[side], right).reshape(4, chunk, 2 * vectors)

    order = (2, 1, 3, 0)

    def of(delta):
        return lax.rem(gx + delta % n_gx, 4)

    sends = {}

    def send_part(src, way, i):
        slot = way * 4 + i
        copy = remote(
            src, recv.at[slot], part_send.at[slot], part_recv.at[slot], 0, DELTAS[i], (0, 2, -2)[way]
        )
        copy.start()
        sends[slot] = copy

    arounds = []
    for k in order:
        part[k] = margin(2 * lax.rem(row_y + k, n_y) + core)
        if k == 2:
            for i in range(4):
                copy = remote(
                    part.at[2, of(DELTAS[i])], around_in.at[i], around_send.at[i], around_recv.at[i], 0, 0, 2 if i < 2 else -2
                )
                copy.start()
                arounds.append(copy)
        elif k == 1:
            send_part(part.at[1, of(DELTAS[3])], 1, 3)
            send_part(part.at[1, of(DELTAS[2])], 1, 2)
        elif k == 3:
            send_part(part.at[3, of(DELTAS[0])], 2, 0)
            send_part(part.at[3, of(DELTAS[1])], 2, 1)
        else:
            for i in (3, 0, 2):
                send_part(part.at[0, of(DELTAS[i])], 0, i)
    if far:
        heard("c")
        tell("d")
    heard("e")
    tell("f")
    for i in (0, 3, 1, 2):
        arounds[i].wait_recv()
        around[i] = part[1 if i < 2 else 3, of(DELTAS[i])] + around_in[i]
        send_part(around.at[i], 1 if i < 2 else 2, i)

    summed = part[0, of(0)]
    for slot in (3, 0, 2, 7, 6, 8, 9, 4, 11, 5, 10):
        sends[slot].wait_recv()
        summed = summed + recv[slot]
    total[...] = summed.reshape(2, chunk // 2, 2 * vectors)

    halves = []
    for i, step in enumerate((2, -2)):
        sub = lax.rem(lax.rem(gx + step % n_gx, n_gx) // 4, 2)
        copy = remote(total.at[sub], half_in.at[i], half_send.at[i], half_recv.at[i], 0, step, 0)
        copy.start()
        halves.append(copy)
    if far:
        heard("d")
    for copy in halves:
        copy.wait_recv()
    window[...] = half_in[0] + half_in[1]
    fars = []
    for i, step in enumerate((12, -12, 4, -4) if far else (4, -4)):
        copy = remote(window, far_in.at[i], far_send.at[i], far_recv.at[i], 0, step, 0)
        copy.start()
        fars.append(copy)
    for copy in fars[::-1]:
        copy.wait_recv()
    final = far_in[0] + far_in[1]
    for i in range(2, len(fars)):
        final = final + far_in[i]
    own = 2 * lax.rem(gx + 2, 4) + lax.rem(gx // 4 + 1, 2)
    every[ta, own] = (final * norm_factor).astype(BF16)

    heard("f")
    lasts = []
    for jt in [i for i in (2, 1, 3, 0) if i < n_ta]:
        for i in (0, 1, 7, 2, 6, 3, 5, 4):
            if jt == 0 and WIDE[i] == 0:
                continue
            slot = jt * 8 + i
            copy = remote(
                every.at[ta, own], every.at[ta, own], last_send.at[slot], last_recv.at[slot], jt, WIDE[i], 0
            )
            copy.start()
            lasts.append(copy)
    locals_[2].wait()
    for copy in lasts:
        copy.wait_recv()

    mine = every[ta].reshape(vectors, 2 * vectors)
    margin_ref[0] = mine[:, :vectors]
    margin_ref[1] = mine[:, vectors:]

    sink = every[pair_ref[0, 0]].reshape(vectors, 2 * vectors)
    source = every[pair_ref[0, 1]].reshape(vectors, 2 * vectors)
    sink_r, sink_i = sink[:, :vectors], sink[:, vectors:]
    source_r, source_i = source[:, :vectors], source[:, vectors:]
    phi = jnp.concatenate(
        [jnp.concatenate([sink_r, -sink_i], axis=1), jnp.concatenate([sink_i, sink_r], axis=1)], axis=0
    )
    psi = jnp.concatenate([source, jnp.concatenate([-source_i, source_r], axis=1)], axis=0)
    spins = tau_ref.shape[1] // vectors
    x_blocks = []
    for s in range(spins):
        rows = pl.ds(s * vectors, vectors)
        x_blocks.append(mm(phi, jnp.concatenate([tau_ref[0, rows, :], tau_ref[1, rows, :]], axis=0)))
    sum_re = jnp.zeros((vectors, vectors), F32)
    sum_im = jnp.zeros((vectors, vectors), F32)
    for t in range(spins):
        cols = pl.ds(t * vectors, vectors)
        y_block = mm_nt(jnp.concatenate([tau_ref[0, :, cols], tau_ref[1, :, cols]], axis=1), psi)
        for s in range(spins):
            x_re = x_blocks[s][:vectors, t * vectors : (t + 1) * vectors]
            x_im = x_blocks[s][vectors:, t * vectors : (t + 1) * vectors]
            y_re = y_block[s * vectors : (s + 1) * vectors, :vectors]
            y_im = y_block[s * vectors : (s + 1) * vectors, vectors:]
            sum_re = sum_re + (x_re * y_re + x_im * y_im)
            sum_im = sum_im + (x_im * y_re - x_re * y_im)
    traces = [jnp.sum(jnp.sum(x, axis=0, keepdims=True), axis=1, keepdims=True) for x in (sum_re, sum_im)]
    part_at = lax.broadcasted_iota(jnp.int32, (1, 2), 1)
    corr_ref[...] = jnp.where(part_at == 0, *traces) / vectors

    for copy in [*halos, passed, *arounds, *sends.values(), *halves, *fars, *lasts]:
        copy.wait_send()

    @pl.when(core == 0)
    def _():
        for copy in edges:
            copy.wait_send()


def solution(mesh):
    sizes = tuple(mesh.shape[axis] for axis in ("ta", "gx", "gy"))

    def per_device(eigvecs, links, op_dirs, op_moms, perams, pair_times, slot_counts):
        cells_x, cells_y, cells_z, colors, parts, vectors = eigvecs.shape[1:]
        rows = cells_x * cells_y * cells_z * colors * parts
        order = perams.shape[-1]
        n_k = 3 * 2 * 3 * 3
        field = eigvecs.reshape(rows, vectors)
        link_rows = links[0, 0].transpose(0, 2, 4, 5, 3, 1).reshape(cells_y, n_k // 2, 2, cells_z)
        norm_factor = 1.0 / math.sqrt(3.0 * cells_x * sizes[1] * cells_y * sizes[2] * cells_z)
        layer = rows // cells_y
        n_far = 4 if sizes[1] >= 32 else 2
        chunk = vectors // 4
        piece = (chunk, 2 * vectors)
        half = (chunk // 2, 2 * vectors)
        tables = [jnp.asarray(t, BF16) for t in selections(cells_z, vectors)] + [jnp.asarray(t, F32) for t in phases(cells_z, vectors)]
        vmem = pl.BlockSpec(memory_space=pltpu.VMEM)
        hbm = pl.BlockSpec(memory_space=pltpu.HBM)
        dma = pltpu.SemaphoreType.DMA
        margins, corr = pl.pallas_call(
            lambda *refs: kernel(sizes, len(tables), norm_factor, *refs),
            name="meson_step",
            out_shape=(
                pltpu.VMEM((2, vectors, vectors), BF16),
                pltpu.VMEM((1, 2), F32),
            ),
            in_specs=[hbm] * (6 + len(tables)),
            out_specs=(vmem, vmem),
            scratch_shapes=[
                *(pltpu.VMEM(table.shape, table.dtype) for table in tables),
                pltpu.VMEM((2, order, order), BF16),
                pltpu.VMEM((2 * rows + layer, vectors), BF16),
                pltpu.VMEM((2, cells_y, n_k // 2, 2, cells_z), BF16),
                pltpu.VMEM((2 * cells_y, 2 * n_k, cells_z), F32),
                pltpu.VMEM((2 * rows, vectors), BF16),
                pltpu.VMEM((7, 2 * rows, vectors), F32),
                pltpu.VMEM((7, 2 * rows, vectors), F32),
                pltpu.VMEM((3, vectors, 2 * rows), BF16),
                pltpu.VMEM((4, 4, *piece), F32),
                pltpu.VMEM((4, *piece), F32),
                pltpu.VMEM((4, *piece), F32),
                pltpu.VMEM((12, *piece), F32),
                pltpu.VMEM((2, *half), F32),
                pltpu.VMEM((2, *half), F32),
                pltpu.VMEM(half, F32),
                pltpu.VMEM((n_far, *half), F32),
                pltpu.VMEM((sizes[0], 8, *half), BF16),
                dma((3,)),
                pltpu.SemaphoreType.REGULAR((12,)),
                dma((8,)),
                dma((7,)),
                dma((4,)),
                dma((4,)),
                dma((12,)),
                dma((12,)),
                dma((2,)),
                dma((2,)),
                dma((n_far,)),
                dma((n_far,)),
                dma((sizes[0] * 8,)),
                dma((sizes[0] * 8,)),
                dma((len(tables),)),
                pltpu.SMEM(op_dirs.shape, jnp.int32),
                pltpu.SMEM(op_moms.shape, jnp.int32),
                pltpu.SMEM(pair_times.shape, jnp.int32),
                dma((3,)),
            ],
            compiler_params=pltpu.CompilerParams(collective_id=0, has_side_effects=True, vmem_limit_bytes=56000 * 1024),
        )(op_dirs, op_moms, pair_times, field, link_rows, perams[0], *tables)
        return margins.astype(F32)[None, None], corr[None]

    placed = (
        P("ta", "gx", "gy", None, None, None, None),
        P("ta", "gx", "gy", None, None, None, None, None),
        P(),
        P(),
        P(("ta", "gx"), None, None, None),
        P(("ta", "gx"), None),
        P(("ta", "gx")),
    )
    return jax.shard_map(
        per_device,
        mesh=mesh,
        in_specs=placed,
        out_specs=(P("ta", "gy", None, None, None), P(("ta", "gx"), "gy", None)),
        check_vma=False,
    )
```
